32 devices in a mesh: gx: 8 (over y, x, core), gy: 4 (over z).
Axes of the slice: x: 2, y: 2, z: 4, core: 2. Of those that a mesh axis runs over, the one named last changes fastest.
Arguments:
- field: bfloat16 [64, 16, 64, 1024], P('gy', None, None, 'gx'), may hold values from -6 to 6
- conv_w: bfloat16 [27, 64, 64], replicated, may hold values from -0.15625 to 0.15625
- spec_re: float32 [16, 64, 64], replicated, may hold values from -6 to 6
- spec_im: float32 [16, 64, 64], replicated, may hold values from -6 to 6
- mlp_in: bfloat16 [256, 64], replicated, may hold values from -0.75 to 0.75
- mlp_out: bfloat16 [64, 256], replicated, may hold values from -0.375 to 0.375
Outputs:
- result: bfloat16 [64, 16, 64, 1024], P('gy', None, None, 'gx')
The draws below stay inside these ranges and needn't reach their ends.
All inputs are finite; a program needn't handle non-finite values.
Results may differ from the reference program's by a relative error of at most 0.0062.
Values may be sent and summed in bfloat16 or wider, within the bound.
A program may use at most 128 MiB of HBM per device.

```python
import math
import jax
import jax.numpy as jnp
from jax import lax

C = 64
HID = 256
MODES = 16
NZ = 16
NX = 1024
NY = 64


def block_levels(rng, dims, shards, least, top_value):
    def one(axis_at, parts):
        heights = jax.random.uniform(jax.random.fold_in(jax.random.fold_in(rng, 6), axis_at), (parts,), jnp.float32, least / len(shards), top_value / len(shards))
        return jnp.repeat(jnp.exp(heights), dims[axis_at] // parts).reshape((-1,) + (1,) * (len(dims) - axis_at - 1))

    loudness = one(*shards[0])
    for cut in shards[1:]:
        loudness = loudness * one(*cut)
    return loudness


def scatter_about(rng, dims, deviation, reach, split=(), held_as=jnp.bfloat16):
    factor_of = block_levels(rng, dims, split, -0.22, 0.18) if split else 1.0
    array = jax.random.normal(rng, dims, jnp.float32) * deviation * factor_of
    return jnp.minimum(jnp.maximum(array, -reach), reach).astype(held_as)


def setup_inputs(seed: int = 0) -> dict:
    arg_keys = jax.random.split(jax.random.key(seed), 7)
    field = scatter_about(arg_keys[0], (NY, NZ, C, NX), 1.0, 6.0, ((0, 4), (3, 8)))
    conv_w = scatter_about(arg_keys[1], (27, C, C), (27 * C) ** -0.5, 0.15625)
    spec_re = scatter_about(arg_keys[2], (MODES, C, C), 1.0, 6.0, (), jnp.float32)
    spec_im = scatter_about(arg_keys[3], (MODES, C, C), 1.0, 6.0, (), jnp.float32)
    mlp_in = scatter_about(arg_keys[4], (HID, C), C ** -0.5, 0.75)
    mlp_out = scatter_about(arg_keys[5], (C, HID), HID ** -0.5, 0.375)
    return {"field": field, "conv_w": conv_w, "spec_re": spec_re, "spec_im": spec_im, "mlp_in": mlp_in, "mlp_out": mlp_out}


def forward_table(start, count, total, modes):
    places = start + jnp.arange(count, dtype=jnp.int32)
    orders = jnp.arange(modes, dtype=jnp.int32)
    phase = (places[:, None] * orders[None, :]) % total
    angle = phase.astype(jnp.float32) * (2.0 * math.pi / total)
    return jnp.concatenate([jnp.cos(angle), -jnp.sin(angle)], axis=1).astype(jnp.bfloat16)


def inverse_table(start, count, total, modes):
    places = start + jnp.arange(count, dtype=jnp.int32)
    orders = jnp.arange(modes, dtype=jnp.int32)
    phase = (orders[:, None] * places[None, :]) % total
    angle = phase.astype(jnp.float32) * (2.0 * math.pi / total)
    scales = jnp.where(orders == 0, 1.0, 2.0).astype(jnp.float32) / total
    return jnp.concatenate([jnp.cos(angle) * scales[:, None], -jnp.sin(angle) * scales[:, None]], axis=0)


def mix_modes(spectrum, spec_re, spec_im):
    modes = spec_re.shape[0]
    real_part = spectrum[..., :modes]
    imag_part = spectrum[..., modes:]
    highest = lax.Precision.HIGHEST
    out_real = jnp.einsum("koc,...ck->...ok", spec_re, real_part, precision=highest) - jnp.einsum("koc,...ck->...ok", spec_im, imag_part, precision=highest)
    out_imag = jnp.einsum("koc,...ck->...ok", spec_re, imag_part, precision=highest) + jnp.einsum("koc,...ck->...ok", spec_im, real_part, precision=highest)
    return jnp.concatenate([out_real, out_imag], axis=-1)


def lift(field, conv_w):
    depth = field.shape[1]
    width = field.shape[3]
    padded = jnp.pad(field, ((1, 1), (1, 1), (0, 0), (1, 1)))
    weights = conv_w.astype(jnp.float32)

    def one_row(row_index):
        slab = lax.dynamic_slice_in_dim(padded, row_index, 3, 0).astype(jnp.float32)
        total = lax.dynamic_index_in_dim(field, row_index, 0, keepdims=False).astype(jnp.float32)
        for shift_y in range(3):
            for shift_z in range(3):
                for shift_x in range(3):
                    tap_index = (shift_y * 3 + shift_z) * 3 + shift_x
                    window = slab[shift_y, shift_z:shift_z + depth, :, shift_x:shift_x + width]
                    total = total + jnp.einsum("oc,zcx->zox", weights[tap_index], window)
        return total.astype(jnp.bfloat16)

    return lax.map(one_row, jnp.arange(field.shape[0], dtype=jnp.int32))


def reference(field, conv_w, spec_re, spec_im, mlp_in, mlp_out):
    lifted = lift(field, conv_w)
    forward = forward_table(0, NX, NX, MODES)
    spectrum = jnp.dot(lifted, forward, preferred_element_type=jnp.float32)
    mixed = mix_modes(spectrum, spec_re, spec_im)
    inverse = inverse_table(0, NX, NX, MODES)
    first_w = mlp_in.astype(jnp.float32)
    second_w = mlp_out.astype(jnp.float32)

    def finish(row_index):
        mixed_row = lax.dynamic_index_in_dim(mixed, row_index, 0, keepdims=False)
        lifted_row = lax.dynamic_index_in_dim(lifted, row_index, 0, keepdims=False)
        branch = jnp.dot(mixed_row, inverse, precision=lax.Precision.HIGHEST)
        blended = (lifted_row.astype(jnp.float32) + branch).astype(jnp.bfloat16)
        hidden = jax.nn.gelu(jnp.einsum("hc,zcx->zhx", first_w, blended.astype(jnp.float32))).astype(jnp.bfloat16)
        down = jnp.einsum("ch,zhx->zcx", second_w, hidden.astype(jnp.float32))
        return (blended.astype(jnp.float32) + down).astype(jnp.bfloat16)

    return lax.map(finish, jnp.arange(NY, dtype=jnp.int32))
```

```python
import functools
import math

import jax
import jax.numpy as jnp
from jax import lax
from jax.experimental import pallas as pl
from jax.experimental.pallas import tpu as pltpu
from jax.sharding import PartitionSpec as P

F32 = jnp.float32
BF16 = jnp.bfloat16
MESH = pl.DeviceIdType.MESH
NT = (((1,), (1,)), ((), ()))
PACK = 4


def kernel(
    n, m, chunks, field, conv_w, spec_re, spec_im, mlp_in, mlp_out, out,
    xs, sh_a, sh_b, carry_a, carry_b, hold, lifted, halo_out, halo_in, edges, up_w, down_w, toep, mixw,
    fwd, inv, part, got, tsum, tmix, mixed, gate, conv_v, re_v, im_v, in_v, out_v,
    load_sem, w_sem, row_send, row_recv, side_send, side_recv, corner_send, corner_recv,
    rs_send, rs_recv, ag_send, ag_recv,
):
    rows, depth, ch, width = field.shape
    modes = spec_re.shape[0]
    total = n * width
    pairs = depth // 2
    crows = rows // chunks
    quads = pairs // PACK
    cgroups = crows * quads
    share = cgroups // n
    per = width // (2 * depth)
    groups = rows // per
    me = lax.axis_index("gx")
    my = lax.axis_index("gy")
    has_left, has_right = me > 0, me < n - 1
    has_up, has_down = my > 0, my < m - 1

    def load(y):
        return pltpu.make_async_copy(
            field.at[y], xs.at[y + 1, pl.ds(1, depth)], load_sem.at[y]
        )

    weights = [(conv_w, conv_v), (spec_re, re_v), (spec_im, im_v), (mlp_in, in_v), (mlp_out, out_v)]

    def fetch(j):
        return pltpu.make_async_copy(weights[j][0], weights[j][1], w_sem.at[j])

    @pl.loop(0, rows)
    def _(y):
        load(y).start()

    for j in range(5):
        fetch(j).start()

    barrier = pltpu.get_barrier_semaphore()

    @pl.loop(1, n)
    def _(o):
        pl.semaphore_signal(
            barrier, inc=1, device_id={"gx": lax.rem(me + o, n)}, device_id_type=MESH
        )

    @pl.when(has_up)
    def _():
        pl.semaphore_signal(barrier, inc=1, device_id={"gy": my - 1}, device_id_type=MESH)

    @pl.when(has_down)
    def _():
        pl.semaphore_signal(barrier, inc=1, device_id={"gy": my + 1}, device_id_type=MESH)

    lane = lax.broadcasted_iota(jnp.int32, (ch, width), 1)

    def pack_edges(g):
        both = jnp.zeros((ch, width), BF16)
        for y in range(per):
            for z in range(depth):
                tile = xs[g * per + y + 1, z + 1]
                to = 2 * (y * depth + z)
                turned = pltpu.roll(tile, to, 1) if to else tile
                hit = (lane == to) | (lane == (to + width - 1) % width)
                both = jnp.where(hit, turned, both)
        halo_out[g] = both

    @pl.loop(0, groups)
    def _(g):
        @pl.loop(0, per)
        def _(y):
            load(g * per + y).wait()

        pack_edges(g)

    pl.semaphore_wait(barrier, n - 1 + has_up.astype(jnp.int32) + has_down.astype(jnp.int32))

    def side_left(g):
        return pltpu.make_async_remote_copy(
            src_ref=halo_out.at[g], dst_ref=halo_in.at[1, g],
            send_sem=side_send.at[0, g], recv_sem=side_recv.at[1, g],
            device_id={"gx": me - 1}, device_id_type=MESH,
        )

    def side_right(g):
        return pltpu.make_async_remote_copy(
            src_ref=halo_out.at[g], dst_ref=halo_in.at[0, g],
            send_sem=side_send.at[1, g], recv_sem=side_recv.at[0, g],
            device_id={"gx": me + 1}, device_id_type=MESH,
        )

    for g in range(groups):
        pl.when(has_left)(lambda g=g: side_left(g).start())
        pl.when(has_right)(lambda g=g: side_right(g).start())

    def row_up():
        return pltpu.make_async_remote_copy(
            src_ref=field.at[0], dst_ref=xs.at[rows + 1, pl.ds(1, depth)],
            send_sem=row_send.at[0], recv_sem=row_recv.at[0],
            device_id={"gy": my - 1}, device_id_type=MESH,
        )

    def row_down():
        return pltpu.make_async_remote_copy(
            src_ref=field.at[rows - 1], dst_ref=xs.at[0, pl.ds(1, depth)],
            send_sem=row_send.at[1], recv_sem=row_recv.at[1],
            device_id={"gy": my + 1}, device_id_type=MESH,
        )

    pl.when(has_up)(lambda: row_up().start())
    pl.when(has_down)(lambda: row_down().start())

    blank = jnp.zeros((ch, width), BF16)

    @pl.loop(0, rows + 2)
    def _(y):
        xs[y, 0] = blank
        xs[y, depth + 1] = blank

    for sh in (sh_a, sh_b):
        for d in range(2):
            sh[d, 0] = blank
            sh[d, depth + 1] = blank

    @pl.when(jnp.logical_not(has_up))
    def _():
        for z in range(depth):
            xs[0, z + 1] = blank
        edges[0] = blank

    @pl.when(jnp.logical_not(has_down))
    def _():
        for z in range(depth):
            xs[rows + 1, z + 1] = blank
        edges[groups + 1] = blank

    @pl.when(jnp.logical_not(has_left))
    def _():
        for g in range(groups):
            halo_in[0, g] = blank

    @pl.when(jnp.logical_not(has_right))
    def _():
        for g in range(groups):
            halo_in[1, g] = blank

    for j in range(5):
        fetch(j).wait()

    up_w[...] = in_v[...].astype(F32).T.astype(BF16)
    down_w[...] = out_v[...] * jnp.asarray(0.5, BF16)

    square = jnp.zeros((ch, ch), BF16)
    for a in range(3):
        for d in range(3):
            taps = [conv_v[(a * 3 + b) * 3 + d] for b in range(3)]
            cols = pl.ds(d * 4 * ch, 4 * ch)
            toep[pl.ds(2 * a * ch, ch), cols] = jnp.concatenate(taps + [square], axis=1)
            toep[pl.ds((2 * a + 1) * ch, ch), cols] = jnp.concatenate([square] + taps, axis=1)

    @pl.loop(0, modes)
    def _(k):
        re = re_v[k].astype(BF16)
        im = im_v[k].astype(BF16)
        mixw[k, 0:ch] = jnp.concatenate([re, -im], axis=1)
        mixw[k, ch:2 * ch] = jnp.concatenate([im, re], axis=1)

    j2 = 2 * modes
    places = me * width + lax.broadcasted_iota(jnp.int32, (j2, width), 1)
    order = lax.broadcasted_iota(jnp.int32, (j2, width), 0)
    k_of = lax.rem(order, modes)
    phase = places * k_of + jnp.where(order >= modes, total // 4, 0)
    wave = jnp.cos(lax.rem(phase, total).astype(F32) * (2.0 * math.pi / total))
    scales = jnp.where(k_of == 0, 1.0, 2.0).astype(F32) / total
    table = wave * scales
    high = table.astype(BF16).astype(F32)
    low_part = table - high
    wide_row = lax.broadcasted_iota(jnp.int32, (PACK * j2, width), 0) // j2
    wide_lane = lax.broadcasted_iota(jnp.int32, (width, PACK * j2), 1) // j2
    columns = jnp.concatenate([wave] * PACK, axis=0).T
    tall = [jnp.concatenate([t] * PACK, axis=0) for t in (high, low_part)]
    for j in range(PACK):
        fwd[j * width:(j + 1) * width] = jnp.where(wide_lane == j, columns, 0.0).astype(BF16)
        for h in range(2):
            inv[h * PACK * j2:(h + 1) * PACK * j2, j * width:(j + 1) * width] = jnp.where(
                wide_row == j, tall[h], 0.0
            ).astype(BF16)

    even = lax.rem(lane, 2) == 0
    for g in range(groups):
        pl.when(has_left)(lambda g=g: side_right(g).wait_recv())
        pl.when(has_right)(lambda g=g: side_left(g).wait_recv())
        edges[g + 1] = jnp.where(even, halo_in[1, g], pltpu.roll(halo_in[0, g], 2, 1))

    def corner_up():
        return pltpu.make_async_remote_copy(
            src_ref=edges.at[1], dst_ref=edges.at[groups + 1],
            send_sem=corner_send.at[0], recv_sem=corner_recv.at[0],
            device_id={"gy": my - 1}, device_id_type=MESH,
        )

    def corner_down():
        return pltpu.make_async_remote_copy(
            src_ref=edges.at[groups], dst_ref=edges.at[0],
            send_sem=corner_send.at[1], recv_sem=corner_recv.at[1],
            device_id={"gy": my + 1}, device_id_type=MESH,
        )

    pl.when(has_up)(lambda: corner_up().start())
    pl.when(has_down)(lambda: corner_down().start())

    def shift_row(i, sh):
        g = (i - 1 + per) // per
        back = lax.rem(i - 1 + per, per) * 2 * depth
        row_edges = pltpu.roll(edges[g], lax.rem(2 * width - 1 - back, width), 1)
        for z in range(depth):
            tile = xs[i, z + 1]
            edge = row_edges if z == 0 else pltpu.roll(row_edges, width - 2 * z, 1)
            sh[0, z + 1] = jnp.where(lane == 0, edge, pltpu.roll(tile, 1, 1))
            sh[1, z + 1] = jnp.where(lane == width - 1, edge, pltpu.roll(tile, width - 1, 1))

    def window(i, sh, d, z):
        at = pl.ds(z, 4)
        tile = xs[i, at] if d == 1 else sh[d // 2, at]
        return tile.reshape(4 * ch, width)

    def conv_row(i, sh, lo, hi, use):
        for q in range(depth // 4):
            rhs = jnp.concatenate(
                [
                    jnp.concatenate([window(i, sh, d, 4 * q), window(i, sh, d, 4 * q + 2)], axis=1)
                    for d in range(3)
                ],
                axis=0,
            )
            acc = jnp.dot(toep[2 * ch * lo:2 * ch * hi], rhs, preferred_element_type=F32)
            use(q, [acc[2 * ch * a:2 * ch * (a + 1)] for a in range(hi - lo)])

    def lift_out(y, q, done):
        for p in range(2):
            own = xs[y + 1, pl.ds(4 * q + 2 * p + 1, 2)].reshape(2 * ch, width)
            lifted[y, 2 * q + p] = (own.astype(F32) + done[:, p * width:(p + 1) * width]).astype(BF16)

    def lift_row(i, sh):
        def use(q, acc):
            lift_out(i - 2, q, carry_b[q] + acc[2])
            carry_b[q] = carry_a[q] + acc[1]
            carry_a[q] = acc[0]

        conv_row(i, sh, 0, 3, use)

    def modes_of(y, slot):
        tiles = jnp.concatenate(
            [
                jnp.concatenate([lifted[y, PACK * g + j] for j in range(PACK)], axis=1)
                for g in range(quads)
            ],
            axis=0,
        )
        res = jnp.dot(tiles, fwd[...], preferred_element_type=F32).astype(BF16)
        for g in range(quads):
            part[slot * quads + g] = res[2 * ch * g:2 * ch * (g + 1)]

    def rs_copy(c, o):
        to = lax.rem(me + o, n)
        return pltpu.make_async_remote_copy(
            src_ref=part.at[pl.ds(c * cgroups + to * share, share)], dst_ref=got.at[c, o],
            send_sem=rs_send.at[c, o], recv_sem=rs_recv.at[c, o],
            device_id={"gx": to}, device_id_type=MESH,
        )

    def ag_copy(c, o):
        mine = pl.ds(c * cgroups + me * share, share)
        return pltpu.make_async_remote_copy(
            src_ref=mixed.at[mine], dst_ref=mixed.at[mine],
            send_sem=ag_send.at[c, o], recv_sem=ag_recv.at[c, o],
            device_id={"gx": lax.rem(me + o, n)}, device_id_type=MESH,
        )

    def ag_wait(c, o):
        theirs = pl.ds(c * cgroups + lax.rem(me + n - o, n) * share, share)
        pltpu.make_async_remote_copy(
            src_ref=mixed.at[theirs], dst_ref=mixed.at[theirs],
            send_sem=ag_send.at[c, o], recv_sem=ag_recv.at[c, o],
            device_id={"gx": lax.rem(me + o, n)}, device_id_type=MESH,
        ).wait_recv()

    half = lax.broadcasted_iota(jnp.int32, (modes, 2 * ch), 1) < ch

    def mix_chunk(c):
        mine = c * cgroups + me * share
        tsum[...] = part[pl.ds(mine, share)].astype(F32)

        @pl.loop(1, n)
        def _(o):
            rs_copy(c, o).wait_recv()
            tsum[...] += got[c, o].astype(F32)

        for s in range(share):
            flat = tsum[s].T
            for j in range(PACK):
                re = flat[j * j2:j * j2 + modes]
                im = flat[j * j2 + modes:(j + 1) * j2]
                tmix[pl.ds(2 * j * modes, modes)] = jnp.where(half, re, pltpu.roll(im, ch, 1))
                tmix[pl.ds((2 * j + 1) * modes, modes)] = jnp.where(half, pltpu.roll(re, ch, 1), im)
            for k in range(modes):
                at = pl.ds(k, 2 * PACK, stride=modes)
                data = tmix[at, :]
                top = data.astype(BF16).astype(F32)
                lhs = jnp.concatenate([top, data - top], axis=0).astype(BF16)
                both = lax.dot_general(lhs, mixw[k], NT, preferred_element_type=F32)
                tmix[at, :] = both[0:2 * PACK] + both[2 * PACK:4 * PACK]
            lines = []
            for j in range(PACK):
                first = tmix[pl.ds(2 * j * modes, modes)]
                second = tmix[pl.ds((2 * j + 1) * modes, modes)]
                lines.append(jnp.where(half, first, pltpu.roll(second, ch, 1)))
                lines.append(jnp.where(half, pltpu.roll(first, ch, 1), second))
            mixed[mine + s] = jnp.concatenate(lines, axis=0).T.astype(BF16)
        pl.loop(1, n)(lambda o: ag_copy(c, o).start())

    slope = math.sqrt(2.0 / math.pi)
    low = jnp.asarray(slope, BF16)
    cubic = jnp.asarray(slope * 0.044715, BF16)

    def row_of(slot):
        return lax.rem(slot + 1, rows)

    def blend(slot):
        y = row_of(slot)
        spec = mixed[pl.ds(slot * quads, quads)].reshape(quads * 2 * ch, width)
        branch = jnp.dot(
            jnp.concatenate([spec, spec], axis=1), inv[...], preferred_element_type=F32
        )
        for g in range(quads):
            for j in range(PACK):
                p = PACK * g + j
                piece = branch[2 * ch * g:2 * ch * (g + 1), j * width:(j + 1) * width]
                lifted[y, p] = (lifted[y, p].astype(F32) + piece).astype(BF16)

    def widen(slot):
        y = row_of(slot)
        for p in range(pairs):
            wide = jnp.concatenate([lifted[y, p, 0:ch], lifted[y, p, ch:2 * ch]], axis=1)
            h = jnp.dot(up_w[...], wide, preferred_element_type=F32).astype(BF16)
            t = jnp.tanh(h * (low + cubic * (h * h)))
            gate[p] = h + h * t

    def narrow(slot):
        y = row_of(slot)
        for p in range(pairs):
            down = jnp.dot(down_w[...], gate[p], preferred_element_type=F32)
            for z in range(2):
                own = lifted[y, p, z * ch:(z + 1) * ch].astype(F32)
                out[y, p, z * ch:(z + 1) * ch] = (
                    own + down[:, z * width:(z + 1) * width]
                ).astype(BF16)

    shift_row(1, sh_a)
    shift_row(2, sh_b)

    def start_first(q, acc):
        carry_a[q] = acc[0]
        hold[q] = acc[1]

    def start_second(q, acc):
        carry_b[q] = carry_a[q] + acc[1]
        carry_a[q] = acc[0]
        hold[q] += acc[2]

    conv_row(1, sh_a, 0, 2, start_first)
    shift_row(3, sh_a)
    conv_row(2, sh_b, 0, 3, start_second)

    def lift_two(i):
        shift_row(i + 1, sh_b)
        lift_row(i, sh_a)
        shift_row(i + 2, sh_a)
        lift_row(i + 1, sh_b)

    def modes_two(i):
        modes_of(i - 2, i - 3)
        modes_of(i - 1, i - 2)

    def lift_last():
        shift_row(0, sh_b)

        def use_bottom(q, acc):
            lift_out(rows - 1, q, carry_b[q] + acc[0])

        def use_top(q, acc):
            lift_out(0, q, hold[q] + acc[0])

        conv_row(rows + 1, sh_a, 2, 3, use_bottom)
        conv_row(0, sh_b, 0, 1, use_top)

    def lift_chunk(c):
        begin = c * crows + 3
        steps = crows // 2 - (c == chunks - 1)
        if steps:
            lift_two(begin)
        if steps > 1:
            @pl.loop(1, steps)
            def _(s):
                modes_two(begin + 2 * s - 2)
                lift_two(begin + 2 * s)
        if c == chunks - 1:
            if steps:
                modes_two(begin + 2 * steps - 2)
            lift_last()
            modes_of(rows - 1, rows - 2)
            modes_of(0, rows - 1)
        else:
            modes_two(begin + 2 * steps - 2)
        pl.loop(1, n)(lambda o: rs_copy(c, o).start())

    def last_layers():
        pl.when(has_up)(lambda: row_down().wait_recv())
        pl.when(has_up)(lambda: corner_down().wait_recv())
        pl.when(has_down)(lambda: row_up().wait_recv())
        pl.when(has_down)(lambda: corner_up().wait_recv())

    for c in range(chunks):
        if c == chunks - 1:
            last_layers()
        lift_chunk(c)
        if c:
            mix_chunk(c - 1)

    def arrive(c):
        pl.loop(1, n)(lambda o: ag_wait(c, o))

    def finish_row(t):
        narrow(t - 2)
        widen(t - 1)
        blend(t)

    if chunks == 1:
        mix_chunk(0)
    arrive(0)
    blend(0)
    widen(0)
    blend(1)
    pl.loop(2, crows)(finish_row)
    for c in range(1, chunks):
        if c == 1:
            mix_chunk(chunks - 1)
        arrive(c)
        pl.loop(c * crows, (c + 1) * crows)(finish_row)
    narrow(rows - 2)
    widen(rows - 1)
    narrow(rows - 1)

    pl.when(has_up)(lambda: row_up().wait_send())
    pl.when(has_down)(lambda: row_down().wait_send())
    pl.when(has_up)(lambda: corner_up().wait_send())
    pl.when(has_down)(lambda: corner_down().wait_send())
    for g in range(groups):
        pl.when(has_left)(lambda g=g: side_left(g).wait_send())
        pl.when(has_right)(lambda g=g: side_right(g).wait_send())
    for c in range(chunks):
        @pl.loop(1, n)
        def _(o):
            rs_copy(c, o).wait_send()
            ag_copy(c, o).wait_send()


def per_device(n, m, field, conv_w, spec_re, spec_im, mlp_in, mlp_out):
    rows, depth, ch, width = field.shape
    modes = spec_re.shape[0]
    pairs = depth // 2
    total_groups = rows * pairs // PACK
    chunks = min(4, total_groups // n)
    share = total_groups // chunks // n
    groups = 2 * rows * depth // width
    dma = pltpu.SemaphoreType.DMA
    hbm = pl.BlockSpec(memory_space=pltpu.HBM)
    tile = (2 * ch, PACK * 2 * modes)
    result = pl.pallas_call(
        functools.partial(kernel, n, m, chunks),
        out_shape=pltpu.VMEM((rows, pairs, 2 * ch, width), BF16),
        in_specs=[hbm] * 6,
        out_specs=pl.BlockSpec(memory_space=pltpu.VMEM),
        scratch_shapes=[
            pltpu.VMEM((rows + 2, depth + 2, ch, width), BF16),
            pltpu.VMEM((2, depth + 2, ch, width), BF16),
            pltpu.VMEM((2, depth + 2, ch, width), BF16),
            pltpu.VMEM((depth // 4, 2 * ch, 2 * width), F32),
            pltpu.VMEM((depth // 4, 2 * ch, 2 * width), F32),
            pltpu.VMEM((depth // 4, 2 * ch, 2 * width), F32),
            pltpu.VMEM((rows, pairs, 2 * ch, width), BF16),
            pltpu.VMEM((groups, ch, width), BF16),
            pltpu.VMEM((2, groups, ch, width), BF16),
            pltpu.VMEM((groups + 2, ch, width), BF16),
            pltpu.VMEM((mlp_in.shape[0], ch), BF16),
            pltpu.VMEM(mlp_out.shape, BF16),
            pltpu.VMEM((6 * ch, 12 * ch), BF16),
            pltpu.VMEM((modes, 2 * ch, 2 * ch), BF16),
            pltpu.VMEM((PACK * width, PACK * 2 * modes), BF16),
            pltpu.VMEM((2 * PACK * 2 * modes, PACK * width), BF16),
            pltpu.VMEM((total_groups,) + tile, BF16),
            pltpu.VMEM((chunks, n, share) + tile, BF16),
            pltpu.VMEM((share,) + tile, F32),
            pltpu.VMEM((PACK * 2 * modes, 2 * ch), F32),
            pltpu.VMEM((total_groups,) + tile, BF16),
            pltpu.VMEM((pairs, mlp_in.shape[0], 2 * width), BF16),
            pltpu.VMEM(conv_w.shape, BF16),
            pltpu.VMEM(spec_re.shape, F32),
            pltpu.VMEM(spec_im.shape, F32),
            pltpu.VMEM(mlp_in.shape[::-1], BF16),
            pltpu.VMEM(mlp_out.shape, BF16),
            dma((rows,)), dma((5,)),
            dma((2,)), dma((2,)),
            dma((2, groups)), dma((2, groups)),
            dma((2,)), dma((2,)),
            dma((chunks, n)), dma((chunks, n)),
            dma((chunks, n)), dma((chunks, n)),
        ],
        compiler_params=pltpu.CompilerParams(
            collective_id=0, has_side_effects=True, vmem_limit_bytes=59 << 20
        ),
    )(field, conv_w, spec_re, spec_im, mlp_in.T, mlp_out)
    return result.reshape(rows, depth, ch, width)


def solution(mesh):
    in_specs = (P("gy", None, None, "gx"), P(), P(), P(), P(), P())
    out_specs = P("gy", None, None, "gx")
    return jax.shard_map(
        functools.partial(per_device, mesh.shape["gx"], mesh.shape["gy"]),
        mesh=mesh, in_specs=in_specs, out_specs=out_specs, check_vma=False,
    )
```

```python
import functools
import math

import jax
import jax.numpy as jnp
from jax import lax
from jax.experimental import pallas as pl
from jax.experimental.pallas import tpu as pltpu
from jax.sharding import PartitionSpec as P

F32 = jnp.float32
BF16 = jnp.bfloat16
MESH = pl.DeviceIdType.MESH
NT = (((1,), (1,)), ((), ()))
PACK = 4
LATER = ((0, 1, 4, 6), (0, 1, 4, 7), (0, 1, 3, 5))


def kernel(
    n, m, chunks, field, conv_w, spec_re, spec_im, mlp_in, mlp_out, out,
    xs, sh_a, sh_b, carry_a, carry_b, hold, lifted, halo_out, halo_in, edges, up_w, down_w, toep, mixw,
    fwd, inv, part, twin, psum, got, tsum, tmix, mixed, blend_a, blend_b, gate_a, gate_b,
    conv_v, re_v, im_v, in_v, out_v,
    load_sem, w_sem, row_send, row_recv, side_send, side_recv, corner_send, corner_recv,
    tw_send, tw_recv, rs_send, rs_recv, ag_send, ag_recv, fw_send, fw_recv,
):
    rows, depth, ch, width = field.shape
    modes = spec_re.shape[0]
    total = n * width
    pairs = depth // 2
    crows = rows // chunks
    quads = pairs // PACK
    cgroups = crows * quads
    share = cgroups // n
    chips = n // 2
    half = cgroups // 2
    per = width // (2 * depth)
    groups = rows // per
    me = lax.axis_index("gx")
    my = lax.axis_index("gy")
    core, chip = lax.rem(me, 2), me // 2
    has_left, has_right = me > 0, me < n - 1
    has_up, has_down = my > 0, my < m - 1

    def load(y):
        return pltpu.make_async_copy(
            field.at[y], xs.at[y + 1, pl.ds(1, depth)], load_sem.at[y]
        )

    weights = [(conv_w, conv_v), (spec_re, re_v), (spec_im, im_v), (mlp_in, in_v), (mlp_out, out_v)]

    def fetch(j):
        return pltpu.make_async_copy(weights[j][0], weights[j][1], w_sem.at[j])

    @pl.loop(0, per)
    def _(y):
        load(y).start()

    fetch(0).start()

    @pl.loop(per, rows)
    def _(y):
        load(y).start()

    for j in range(1, 5):
        fetch(j).start()

    barrier = pltpu.get_barrier_semaphore()

    @pl.loop(1, n)
    def _(o):
        pl.semaphore_signal(
            barrier, inc=1, device_id={"gx": lax.rem(me + o, n)}, device_id_type=MESH
        )

    @pl.when(has_up)
    def _():
        pl.semaphore_signal(barrier, inc=1, device_id={"gy": my - 1}, device_id_type=MESH)

    @pl.when(has_down)
    def _():
        pl.semaphore_signal(barrier, inc=1, device_id={"gy": my + 1}, device_id_type=MESH)

    lane = lax.broadcasted_iota(jnp.int32, (ch, width), 1)

    def pack_edges(g):
        both = jnp.zeros((ch, width), BF16)
        for y in range(per):
            for z in range(depth):
                tile = xs[g * per + y + 1, z + 1]
                to = 2 * (y * depth + z)
                turned = pltpu.roll(tile, to, 1) if to else tile
                hit = (lane == to) | (lane == (to + width - 1) % width)
                both = jnp.where(hit, turned, both)
        halo_out[g] = both

    def side_left(g):
        return pltpu.make_async_remote_copy(
            src_ref=halo_out.at[g], dst_ref=halo_in.at[1, g],
            send_sem=side_send.at[0, g], recv_sem=side_recv.at[1, g],
            device_id={"gx": me - 1}, device_id_type=MESH,
        )

    def side_right(g):
        return pltpu.make_async_remote_copy(
            src_ref=halo_out.at[g], dst_ref=halo_in.at[0, g],
            send_sem=side_send.at[1, g], recv_sem=side_recv.at[0, g],
            device_id={"gx": me + 1}, device_id_type=MESH,
        )

    def row_up():
        return pltpu.make_async_remote_copy(
            src_ref=field.at[0], dst_ref=xs.at[rows + 1, pl.ds(1, depth)],
            send_sem=row_send.at[0], recv_sem=row_recv.at[0],
            device_id={"gy": my - 1}, device_id_type=MESH,
        )

    def row_down():
        return pltpu.make_async_remote_copy(
            src_ref=field.at[rows - 1], dst_ref=xs.at[0, pl.ds(1, depth)],
            send_sem=row_send.at[1], recv_sem=row_recv.at[1],
            device_id={"gy": my + 1}, device_id_type=MESH,
        )

    def send_edges(g):
        @pl.loop(0, per)
        def _(y):
            load(g * per + y).wait()

        pack_edges(g)

    def start_sides(g):
        pl.when(has_left)(lambda: side_left(g).start())
        pl.when(has_right)(lambda: side_right(g).start())

    blank = jnp.zeros((ch, width), BF16)

    @pl.loop(0, rows + 2)
    def _(y):
        xs[y, 0] = blank
        xs[y, depth + 1] = blank

    for sh in (sh_a, sh_b):
        for d in range(2):
            sh[d, 0] = blank
            sh[d, depth + 1] = blank

    @pl.when(jnp.logical_not(has_up))
    def _():
        for z in range(depth):
            xs[0, z + 1] = blank
        edges[0] = blank

    @pl.when(jnp.logical_not(has_down))
    def _():
        for z in range(depth):
            xs[rows + 1, z + 1] = blank
        edges[groups + 1] = blank

    @pl.when(jnp.logical_not(has_left))
    def _():
        for g in range(groups):
            halo_in[0, g] = blank

    @pl.when(jnp.logical_not(has_right))
    def _():
        for g in range(groups):
            halo_in[1, g] = blank

    send_edges(0)
    pl.semaphore_wait(barrier, n - 1 + has_up.astype(jnp.int32) + has_down.astype(jnp.int32))
    start_sides(0)

    @pl.loop(1, groups)
    def _(g):
        send_edges(g)
        start_sides(g)

    pl.when(has_up)(lambda: row_up().start())
    pl.when(has_down)(lambda: row_down().start())

    for j in range(5):
        fetch(j).wait()

    up_w[...] = in_v[...].astype(F32).T.astype(BF16)
    down_w[...] = out_v[...] * jnp.asarray(0.5, BF16)

    square = jnp.zeros((ch, ch), BF16)
    for a in range(3):
        for d in range(3):
            taps = [conv_v[(a * 3 + b) * 3 + d] for b in range(3)]
            cols = pl.ds(d * 4 * ch, 4 * ch)
            toep[pl.ds(2 * a * ch, ch), cols] = jnp.concatenate(taps + [square], axis=1)
            toep[pl.ds((2 * a + 1) * ch, ch), cols] = jnp.concatenate([square] + taps, axis=1)

    def mix_weights():
        for k in range(modes):
            re = re_v[k].astype(BF16)
            im = im_v[k].astype(BF16)
            mixw[k, 0:ch] = jnp.concatenate([re, -im], axis=1)
            mixw[k, ch:2 * ch] = jnp.concatenate([im, re], axis=1)

    j2 = 2 * modes
    places = me * width + lax.broadcasted_iota(jnp.int32, (j2, width), 1)
    order = lax.broadcasted_iota(jnp.int32, (j2, width), 0)
    k_of = lax.rem(order, modes)
    phase = places * k_of + jnp.where(order >= modes, total // 4, 0)
    wave = jnp.cos(lax.rem(phase, total).astype(F32) * (2.0 * math.pi / total))
    scales = jnp.where(k_of == 0, 1.0, 2.0).astype(F32) / total
    table = wave * scales
    high = table.astype(BF16).astype(F32)
    low_part = table - high
    wide_row = lax.broadcasted_iota(jnp.int32, (PACK * j2, width), 0) // j2
    wide_lane = lax.broadcasted_iota(jnp.int32, (width, PACK * j2), 1) // j2
    columns = jnp.concatenate([wave] * PACK, axis=0).T
    tall = [jnp.concatenate([t] * PACK, axis=0) for t in (high, low_part)]
    for j in range(PACK):
        fwd[j * width:(j + 1) * width] = jnp.where(wide_lane == j, columns, 0.0).astype(BF16)
        for h in range(2):
            inv[h * PACK * j2:(h + 1) * PACK * j2, j * width:(j + 1) * width] = jnp.where(
                wide_row == j, tall[h], 0.0
            ).astype(BF16)

    even = lax.rem(lane, 2) == 0
    def join_edges(g):
        pl.when(has_left)(lambda: side_right(g).wait_recv())
        pl.when(has_right)(lambda: side_left(g).wait_recv())
        edges[g + 1] = jnp.where(even, halo_in[1, g], pltpu.roll(halo_in[0, g], 2, 1))
        if g == 0:
            pl.when(has_up)(lambda: corner_up().start())
        if g == groups - 1:
            pl.when(has_down)(lambda: corner_down().start())

    def corner_up():
        return pltpu.make_async_remote_copy(
            src_ref=edges.at[1], dst_ref=edges.at[groups + 1],
            send_sem=corner_send.at[0], recv_sem=corner_recv.at[0],
            device_id={"gy": my - 1}, device_id_type=MESH,
        )

    def corner_down():
        return pltpu.make_async_remote_copy(
            src_ref=edges.at[groups], dst_ref=edges.at[0],
            send_sem=corner_send.at[1], recv_sem=corner_recv.at[1],
            device_id={"gy": my + 1}, device_id_type=MESH,
        )

    def shift_row(i, sh):
        g = (i - 1 + per) // per
        back = lax.rem(i - 1 + per, per) * 2 * depth
        row_edges = pltpu.roll(edges[g], lax.rem(2 * width - 1 - back, width), 1)
        for z in range(depth):
            tile = xs[i, z + 1]
            edge = row_edges if z == 0 else pltpu.roll(row_edges, width - 2 * z, 1)
            sh[0, z + 1] = jnp.where(lane == 0, edge, pltpu.roll(tile, 1, 1))
            sh[1, z + 1] = jnp.where(lane == width - 1, edge, pltpu.roll(tile, width - 1, 1))

    def window(i, sh, d, z):
        at = pl.ds(z, 4)
        tile = xs[i, at] if d == 1 else sh[d // 2, at]
        return tile.reshape(4 * ch, width)

    def conv_row(i, sh, lo, hi, use):
        for q in range(depth // 4):
            rhs = jnp.concatenate(
                [
                    jnp.concatenate([window(i, sh, d, 4 * q), window(i, sh, d, 4 * q + 2)], axis=1)
                    for d in range(3)
                ],
                axis=0,
            )
            acc = jnp.dot(toep[2 * ch * lo:2 * ch * hi], rhs, preferred_element_type=F32)
            use(q, [acc[2 * ch * a:2 * ch * (a + 1)] for a in range(hi - lo)])

    def lift_out(y, q, done):
        for p in range(2):
            own = xs[y + 1, pl.ds(4 * q + 2 * p + 1, 2)].reshape(2 * ch, width)
            lifted[y, 2 * q + p] = (own.astype(F32) + done[:, p * width:(p + 1) * width]).astype(BF16)

    def lift_row(i, sh):
        def use(q, acc):
            lift_out(i - 2, q, carry_b[q] + acc[2])
            carry_b[q] = carry_a[q] + acc[1]
            carry_a[q] = acc[0]

        conv_row(i, sh, 0, 3, use)

    def modes_of(y, slot):
        tiles = jnp.concatenate(
            [
                jnp.concatenate([lifted[y, PACK * g + j] for j in range(PACK)], axis=1)
                for g in range(quads)
            ],
            axis=0,
        )
        res = jnp.dot(tiles, fwd[...], preferred_element_type=F32).astype(BF16)
        for g in range(quads):
            part[slot * quads + g] = res[2 * ch * g:2 * ch * (g + 1)]

    def mine(c):
        return c * cgroups + core * half + chip * share

    def peer(o):
        return {"gx": 2 * lax.rem(chip + o, chips) + core}

    def tw_copy(c):
        return pltpu.make_async_remote_copy(
            src_ref=part.at[pl.ds(c * cgroups + (1 - core) * half, half)], dst_ref=twin.at[c],
            send_sem=tw_send.at[c], recv_sem=tw_recv.at[c],
            device_id={"gx": me + 1 - 2 * core}, device_id_type=MESH,
        )

    def rs_copy(c, o):
        return pltpu.make_async_remote_copy(
            src_ref=psum.at[c, pl.ds(lax.rem(chip + o, chips) * share, share)], dst_ref=got.at[c, o],
            send_sem=rs_send.at[c, o], recv_sem=rs_recv.at[c, o],
            device_id=peer(o), device_id_type=MESH,
        )

    def ag_copy(c, o):
        at = pl.ds(mine(c), share)
        return pltpu.make_async_remote_copy(
            src_ref=mixed.at[at], dst_ref=mixed.at[at],
            send_sem=ag_send.at[c, o], recv_sem=ag_recv.at[c, o],
            device_id=peer(o), device_id_type=MESH,
        )

    def ag_wait(c, o):
        at = pl.ds(c * cgroups + core * half + lax.rem(chip + chips - o, chips) * share, share)
        pltpu.make_async_remote_copy(
            src_ref=mixed.at[at], dst_ref=mixed.at[at],
            send_sem=ag_send.at[c, o], recv_sem=ag_recv.at[c, o],
            device_id=peer(o), device_id_type=MESH,
        ).wait_recv()

    def fw_copy(c, which):
        at = pl.ds(c * cgroups + which * half, half)
        return pltpu.make_async_remote_copy(
            src_ref=mixed.at[at], dst_ref=mixed.at[at],
            send_sem=fw_send.at[c], recv_sem=fw_recv.at[c],
            device_id={"gx": me + 1 - 2 * core}, device_id_type=MESH,
        )

    def to_twin(c):
        tw_copy(c).start()

    def to_peers(c):
        tw_copy(c).wait_recv()
        own = part[pl.ds(c * cgroups + core * half, half)]
        psum[c] = (own.astype(F32) + twin[c].astype(F32)).astype(BF16)
        pl.loop(1, chips)(lambda o: rs_copy(c, o).start())

    def forward(c):
        pl.loop(1, chips)(lambda o: ag_wait(c, o))
        fw_copy(c, core).start()

    front = lax.broadcasted_iota(jnp.int32, (modes, 2 * ch), 1) < ch

    def mix_chunk(c):
        tsum[...] = psum[c, pl.ds(chip * share, share)].astype(F32)

        @pl.loop(1, chips)
        def _(o):
            rs_copy(c, o).wait_recv()
            tsum[...] += got[c, o].astype(F32)

        for s in range(share):
            flat = tsum[s].T
            for j in range(PACK):
                re = flat[j * j2:j * j2 + modes]
                im = flat[j * j2 + modes:(j + 1) * j2]
                tmix[pl.ds(2 * j * modes, modes)] = jnp.where(front, re, pltpu.roll(im, ch, 1))
                tmix[pl.ds((2 * j + 1) * modes, modes)] = jnp.where(front, pltpu.roll(re, ch, 1), im)
            for k in range(modes):
                at = pl.ds(k, 2 * PACK, stride=modes)
                data = tmix[at, :]
                top = data.astype(BF16).astype(F32)
                lhs = jnp.concatenate([top, data - top], axis=0).astype(BF16)
                both = lax.dot_general(lhs, mixw[k], NT, preferred_element_type=F32)
                tmix[at, :] = both[0:2 * PACK] + both[2 * PACK:4 * PACK]
            lines = []
            for j in range(PACK):
                first = tmix[pl.ds(2 * j * modes, modes)]
                second = tmix[pl.ds((2 * j + 1) * modes, modes)]
                lines.append(jnp.where(front, first, pltpu.roll(second, ch, 1)))
                lines.append(jnp.where(front, pltpu.roll(first, ch, 1), second))
            mixed[mine(c) + s] = jnp.concatenate(lines, axis=0).T.astype(BF16)
        pl.loop(1, chips)(lambda o: ag_copy(c, o).start())

    slope = math.sqrt(2.0 / math.pi)
    low = jnp.asarray(slope, BF16)
    cubic = jnp.asarray(slope * 0.044715, BF16)

    def row_of(slot):
        return lax.rem(slot + 1, rows)

    def blend(slot, to):
        y = row_of(slot)
        spec = mixed[pl.ds(slot * quads, quads)].reshape(quads * 2 * ch, width)
        branch = jnp.dot(
            jnp.concatenate([spec, spec], axis=1), inv[...], preferred_element_type=F32
        )
        for g in range(quads):
            for j in range(PACK):
                p = PACK * g + j
                piece = branch[2 * ch * g:2 * ch * (g + 1), j * width:(j + 1) * width]
                to[p] = (lifted[y, p].astype(F32) + piece).astype(BF16)

    def widen(own, gate):
        for p in range(pairs):
            wide = jnp.concatenate([own[p, 0:ch], own[p, ch:2 * ch]], axis=1)
            h = jnp.dot(up_w[...], wide, preferred_element_type=F32).astype(BF16)
            t = jnp.tanh(h * (low + cubic * (h * h)))
            g = h + h * t
            gate[2 * p] = g[:, :width]
            gate[2 * p + 1] = g[:, width:]

    def narrow(slot, own, gate):
        y = row_of(slot)
        for p in range(pairs):
            g = jnp.concatenate([gate[2 * p], gate[2 * p + 1]], axis=1)
            down = jnp.dot(down_w[...], g, preferred_element_type=F32)
            for z in range(2):
                at = pl.ds(z * ch, ch)
                out[y, p, at] = (
                    own[p, at].astype(F32) + down[:, z * width:(z + 1) * width]
                ).astype(BF16)

    join_edges(0)
    if per < 5:
        join_edges(1)
    shift_row(1, sh_a)
    shift_row(2, sh_b)

    def start_first(q, acc):
        carry_a[q] = acc[0]
        hold[q] = acc[1]

    def start_second(q, acc):
        carry_b[q] = carry_a[q] + acc[1]
        carry_a[q] = acc[0]
        hold[q] += acc[2]

    conv_row(1, sh_a, 0, 2, start_first)
    shift_row(3, sh_a)
    conv_row(2, sh_b, 0, 3, start_second)

    def lift_two(i):
        shift_row(i + 1, sh_b)
        lift_row(i, sh_a)
        shift_row(i + 2, sh_a)
        lift_row(i + 1, sh_b)

    def modes_two(i):
        modes_of(i - 2, i - 3)
        modes_of(i - 1, i - 2)

    def lift_last():
        shift_row(0, sh_b)

        def use_bottom(q, acc):
            lift_out(rows - 1, q, carry_b[q] + acc[0])

        def use_top(q, acc):
            lift_out(0, q, hold[q] + acc[0])

        conv_row(rows + 1, sh_a, 2, 3, use_bottom)
        conv_row(0, sh_b, 0, 1, use_top)

    def last_layers():
        pl.when(has_up)(lambda: row_down().wait_recv())
        pl.when(has_up)(lambda: corner_down().wait_recv())
        pl.when(has_down)(lambda: row_up().wait_recv())
        pl.when(has_down)(lambda: corner_up().wait_recv())

    lifts = rows // 2 - 1
    span = crows // 2
    after = {}

    def book(at, call):
        after.setdefault(at, []).append(call)

    for s in range(1, lifts):
        for g in range(1, groups):
            if (4 + 2 * (s - 1)) // per < g <= (4 + 2 * s) // per:
                book(s - 1, functools.partial(join_edges, g))
    book(lifts - 2, last_layers)
    for c in range(chunks):
        at = min((c + 1) * span - 1, lifts) if c < chunks - 1 else lifts
        due = lifts + c * span
        for call, later in zip((to_twin, to_peers, mix_chunk, forward), LATER[min(c, 1) + (c == chunks - 1)]):
            book(min(at + later, due), functools.partial(call, c))

    def then(at):
        for call in after.get(at, []):
            call()

    def lift_step(s, first, last):
        if not first:
            modes_two(2 * s + 1)
        lift_two(2 * s + 3)
        if last:
            modes_two(2 * s + 3)

    mix_weights()
    if chunks > 1:
        for s in range(lifts):
            lift_step(s, s % span == 0, s % span == span - 1)
            then(s)
        if lifts % span:
            modes_two(2 * lifts + 1)
    else:
        lift_step(0, True, False)
        then(0)

        @pl.loop(1, lifts)
        def _(s):
            lift_step(s, False, False)
            for at in range(1, lifts):
                if at in after:
                    pl.when(s == at)(lambda at=at: then(at))

        modes_two(2 * lifts + 1)
    lift_last()
    modes_of(rows - 1, rows - 2)
    modes_of(0, rows - 1)
    then(lifts)

    def arrive(c):
        fw_copy(c, 1 - core).wait_recv()

    arrive(0)
    blend(0, blend_a)
    widen(blend_a, gate_a)
    blend(1, blend_b)
    then(lifts + 1)

    @pl.loop(1, rows // 2)
    def _(s):
        if chunks > 1:
            pl.when(lax.rem(s, span) == 0)(lambda: arrive(s // span))
        t = 2 * s
        narrow(t - 2, blend_a, gate_a)
        widen(blend_b, gate_b)
        blend(t, blend_a)
        narrow(t - 1, blend_b, gate_b)
        widen(blend_a, gate_a)
        blend(t + 1, blend_b)
        for at in range(1, rows // 2):
            if lifts + 1 + at in after:
                pl.when(s == at)(lambda at=at: then(lifts + 1 + at))

    narrow(rows - 2, blend_a, gate_a)
    widen(blend_b, gate_b)
    narrow(rows - 1, blend_b, gate_b)

    pl.when(has_up)(lambda: row_up().wait_send())
    pl.when(has_down)(lambda: row_down().wait_send())
    pl.when(has_up)(lambda: corner_up().wait_send())
    pl.when(has_down)(lambda: corner_down().wait_send())
    for g in range(groups):
        pl.when(has_left)(lambda g=g: side_left(g).wait_send())
        pl.when(has_right)(lambda g=g: side_right(g).wait_send())
    for c in range(chunks):
        tw_copy(c).wait_send()
        fw_copy(c, core).wait_send()

        @pl.loop(1, chips)
        def _(o):
            rs_copy(c, o).wait_send()
            ag_copy(c, o).wait_send()


def per_device(n, m, field, conv_w, spec_re, spec_im, mlp_in, mlp_out):
    rows, depth, ch, width = field.shape
    modes = spec_re.shape[0]
    pairs = depth // 2
    total_groups = rows * pairs // PACK
    chunks = min(4, total_groups // n)
    share = total_groups // chunks // n
    groups = 2 * rows * depth // width
    dma = pltpu.SemaphoreType.DMA
    hbm = pl.BlockSpec(memory_space=pltpu.HBM)
    tile = (2 * ch, PACK * 2 * modes)
    result = pl.pallas_call(
        functools.partial(kernel, n, m, chunks),
        out_shape=pltpu.VMEM((rows, pairs, 2 * ch, width), BF16),
        in_specs=[hbm] * 6,
        out_specs=pl.BlockSpec(memory_space=pltpu.VMEM),
        scratch_shapes=[
            pltpu.VMEM((rows + 2, depth + 2, ch, width), BF16),
            pltpu.VMEM((2, depth + 2, ch, width), BF16),
            pltpu.VMEM((2, depth + 2, ch, width), BF16),
            pltpu.VMEM((depth // 4, 2 * ch, 2 * width), F32),
            pltpu.VMEM((depth // 4, 2 * ch, 2 * width), F32),
            pltpu.VMEM((depth // 4, 2 * ch, 2 * width), F32),
            pltpu.VMEM((rows, pairs, 2 * ch, width), BF16),
            pltpu.VMEM((groups, ch, width), BF16),
            pltpu.VMEM((2, groups, ch, width), BF16),
            pltpu.VMEM((groups + 2, ch, width), BF16),
            pltpu.VMEM((mlp_in.shape[0], ch), BF16),
            pltpu.VMEM(mlp_out.shape, BF16),
            pltpu.VMEM((6 * ch, 12 * ch), BF16),
            pltpu.VMEM((modes, 2 * ch, 2 * ch), BF16),
            pltpu.VMEM((PACK * width, PACK * 2 * modes), BF16),
            pltpu.VMEM((2 * PACK * 2 * modes, PACK * width), BF16),
            pltpu.VMEM((total_groups,) + tile, BF16),
            pltpu.VMEM((chunks, total_groups // chunks // 2) + tile, BF16),
            pltpu.VMEM((chunks, total_groups // chunks // 2) + tile, BF16),
            pltpu.VMEM((chunks, n // 2, share) + tile, BF16),
            pltpu.VMEM((share,) + tile, F32),
            pltpu.VMEM((PACK * 2 * modes, 2 * ch), F32),
            pltpu.VMEM((total_groups,) + tile, BF16),
            pltpu.VMEM((pairs, 2 * ch, width), BF16),
            pltpu.VMEM((pairs, 2 * ch, width), BF16),
            pltpu.VMEM((depth, mlp_in.shape[0], width), BF16),
            pltpu.VMEM((depth, mlp_in.shape[0], width), BF16),
            pltpu.VMEM(conv_w.shape, BF16),
            pltpu.VMEM(spec_re.shape, F32),
            pltpu.VMEM(spec_im.shape, F32),
            pltpu.VMEM(mlp_in.shape[::-1], BF16),
            pltpu.VMEM(mlp_out.shape, BF16),
            dma((rows,)), dma((5,)),
            dma((2,)), dma((2,)),
            dma((2, groups)), dma((2, groups)),
            dma((2,)), dma((2,)),
            dma((chunks,)), dma((chunks,)),
            dma((chunks, n // 2)), dma((chunks, n // 2)),
            dma((chunks, n // 2)), dma((chunks, n // 2)),
            dma((chunks,)), dma((chunks,)),
        ],
        compiler_params=pltpu.CompilerParams(
            collective_id=0, has_side_effects=True, vmem_limit_bytes=59 << 20
        ),
    )(field, conv_w, spec_re, spec_im, mlp_in.T, mlp_out)
    return result.reshape(rows, depth, ch, width)


def solution(mesh):
    in_specs = (P("gy", None, None, "gx"), P(), P(), P(), P(), P())
    out_specs = P("gy", None, None, "gx")
    return jax.shard_map(
        functools.partial(per_device, mesh.shape["gx"], mesh.shape["gy"]),
        mesh=mesh, in_specs=in_specs, out_specs=out_specs, check_vma=False,
    )
```

```python
import functools
import math

import jax
import jax.numpy as jnp
from jax import lax
from jax.experimental import pallas as pl
from jax.experimental.pallas import tpu as pltpu
from jax.sharding import PartitionSpec as P

F32 = jnp.float32
BF16 = jnp.bfloat16
MESH = pl.DeviceIdType.MESH
NT = (((1,), (1,)), ((), ()))
PACK = 4
LATER = ((0, 1, 4, 6), (0, 1, 4, 5), (0, 1, 3, 5), (0, 0, 2, 5))
RANKS = {"to_twin": 0, "to_peers": 1, "mix_chunk": 2, "forward": 3}


def kernel(
    n, m, chunks, field, conv_w, spec_re, spec_im, mlp_in, mlp_out, out,
    xs, sh_a, sh_b, carry_a, carry_b, hold, lifted, halo_out, halo_in, edges, up_w, down_w, toep, mixw,
    fwd, inv, part, twin, psum, got, tsum, tmix, mixed, blend_a, blend_b, gate_a, gate_b,
    conv_v, re_v, im_v, in_v, out_v,
    load_sem, w_sem, row_send, row_recv, side_send, side_recv, corner_send, corner_recv,
    tw_send, tw_recv, rs_send, rs_recv, ag_send, ag_recv, fw_send, fw_recv,
):
    rows, depth, ch, width = field.shape
    modes = spec_re.shape[0]
    total = n * width
    pairs = depth // 2
    crows = rows // chunks
    quads = pairs // PACK
    cgroups = crows * quads
    share = cgroups // n
    chips = n // 2
    half = cgroups // 2
    per = width // (2 * depth)
    groups = rows // per
    me = lax.axis_index("gx")
    my = lax.axis_index("gy")
    core, chip = lax.rem(me, 2), me // 2
    has_left, has_right = me > 0, me < n - 1
    has_up, has_down = my > 0, my < m - 1

    def load(y):
        return pltpu.make_async_copy(
            field.at[y], xs.at[y + 1, pl.ds(1, depth)], load_sem.at[y]
        )

    weights = [(conv_w, conv_v), (spec_re, re_v), (spec_im, im_v), (mlp_in, in_v), (mlp_out, out_v)]

    def fetch(j):
        return pltpu.make_async_copy(weights[j][0], weights[j][1], w_sem.at[j])

    @pl.loop(0, per)
    def _(y):
        load(y).start()

    fetch(0).start()

    @pl.loop(per, rows)
    def _(y):
        load(y).start()

    for j in range(1, 5):
        fetch(j).start()

    barrier = pltpu.get_barrier_semaphore()

    @pl.loop(1, n)
    def _(o):
        pl.semaphore_signal(
            barrier, inc=1, device_id={"gx": lax.rem(me + o, n)}, device_id_type=MESH
        )

    @pl.when(has_up)
    def _():
        pl.semaphore_signal(barrier, inc=1, device_id={"gy": my - 1}, device_id_type=MESH)

    @pl.when(has_down)
    def _():
        pl.semaphore_signal(barrier, inc=1, device_id={"gy": my + 1}, device_id_type=MESH)

    lane = lax.broadcasted_iota(jnp.int32, (ch, width), 1)

    def pack_edges(g):
        both = jnp.zeros((ch, width), BF16)
        for y in range(per):
            for z in range(depth):
                tile = xs[g * per + y + 1, z + 1]
                to = 2 * (y * depth + z)
                turned = pltpu.roll(tile, to, 1) if to else tile
                hit = (lane == to) | (lane == (to + width - 1) % width)
                both = jnp.where(hit, turned, both)
        halo_out[g] = both

    def side_left(g):
        return pltpu.make_async_remote_copy(
            src_ref=halo_out.at[g], dst_ref=halo_in.at[1, g],
            send_sem=side_send.at[0, g], recv_sem=side_recv.at[1, g],
            device_id={"gx": me - 1}, device_id_type=MESH,
        )

    def side_right(g):
        return pltpu.make_async_remote_copy(
            src_ref=halo_out.at[g], dst_ref=halo_in.at[0, g],
            send_sem=side_send.at[1, g], recv_sem=side_recv.at[0, g],
            device_id={"gx": me + 1}, device_id_type=MESH,
        )

    def row_up():
        return pltpu.make_async_remote_copy(
            src_ref=field.at[0], dst_ref=xs.at[rows + 1, pl.ds(1, depth)],
            send_sem=row_send.at[0], recv_sem=row_recv.at[0],
            device_id={"gy": my - 1}, device_id_type=MESH,
        )

    def row_down():
        return pltpu.make_async_remote_copy(
            src_ref=field.at[rows - 1], dst_ref=xs.at[0, pl.ds(1, depth)],
            send_sem=row_send.at[1], recv_sem=row_recv.at[1],
            device_id={"gy": my + 1}, device_id_type=MESH,
        )

    def send_edges(g):
        @pl.loop(0, per)
        def _(y):
            load(g * per + y).wait()

        pack_edges(g)

    def start_sides(g):
        pl.when(has_left)(lambda: side_left(g).start())
        pl.when(has_right)(lambda: side_right(g).start())

    blank = jnp.zeros((ch, width), BF16)

    @pl.loop(0, rows + 2)
    def _(y):
        xs[y, 0] = blank
        xs[y, depth + 1] = blank

    for sh in (sh_a, sh_b):
        for d in range(2):
            sh[d, 0] = blank
            sh[d, depth + 1] = blank

    @pl.when(jnp.logical_not(has_up))
    def _():
        for z in range(depth):
            xs[0, z + 1] = blank
        edges[0] = blank

    @pl.when(jnp.logical_not(has_down))
    def _():
        for z in range(depth):
            xs[rows + 1, z + 1] = blank
        edges[groups + 1] = blank

    @pl.when(jnp.logical_not(has_left))
    def _():
        for g in range(groups):
            halo_in[0, g] = blank

    @pl.when(jnp.logical_not(has_right))
    def _():
        for g in range(groups):
            halo_in[1, g] = blank

    send_edges(0)
    pl.semaphore_wait(barrier, n - 1 + has_up.astype(jnp.int32) + has_down.astype(jnp.int32))
    start_sides(0)

    @pl.loop(1, groups)
    def _(g):
        send_edges(g)
        start_sides(g)

    pl.when(has_up)(lambda: row_up().start())
    pl.when(has_down)(lambda: row_down().start())

    for j in range(5):
        fetch(j).wait()

    up_w[...] = in_v[...].astype(F32).T.astype(BF16)
    down_w[...] = out_v[...] * jnp.asarray(0.5, BF16)

    square = jnp.zeros((ch, ch), BF16)
    for a in range(3):
        for d in range(3):
            taps = [conv_v[(a * 3 + b) * 3 + d] for b in range(3)]
            cols = pl.ds(d * 4 * ch, 4 * ch)
            toep[pl.ds(2 * a * ch, ch), cols] = jnp.concatenate(taps + [square], axis=1)
            toep[pl.ds((2 * a + 1) * ch, ch), cols] = jnp.concatenate([square] + taps, axis=1)

    def mix_weights():
        for k in range(modes):
            re = re_v[k].astype(BF16)
            im = im_v[k].astype(BF16)
            mixw[k, 0:ch] = jnp.concatenate([re, -im], axis=1)
            mixw[k, ch:2 * ch] = jnp.concatenate([im, re], axis=1)

    j2 = 2 * modes
    places = me * width + lax.broadcasted_iota(jnp.int32, (j2, width), 1)
    order = lax.broadcasted_iota(jnp.int32, (j2, width), 0)
    k_of = lax.rem(order, modes)
    phase = places * k_of + jnp.where(order >= modes, total // 4, 0)
    wave = jnp.cos(lax.rem(phase, total).astype(F32) * (2.0 * math.pi / total))
    scales = jnp.where(k_of == 0, 1.0, 2.0).astype(F32) / total
    table = wave * scales
    high = table.astype(BF16).astype(F32)
    low_part = table - high
    wide_row = lax.broadcasted_iota(jnp.int32, (PACK * j2, width), 0) // j2
    wide_lane = lax.broadcasted_iota(jnp.int32, (width, PACK * j2), 1) // j2
    columns = jnp.concatenate([wave] * PACK, axis=0).T
    tall = [jnp.concatenate([t] * PACK, axis=0) for t in (high, low_part)]
    for j in range(PACK):
        fwd[j * width:(j + 1) * width] = jnp.where(wide_lane == j, columns, 0.0).astype(BF16)
        for h in range(2):
            inv[h * PACK * j2:(h + 1) * PACK * j2, j * width:(j + 1) * width] = jnp.where(
                wide_row == j, tall[h], 0.0
            ).astype(BF16)

    even = lax.rem(lane, 2) == 0
    def join_edges(g):
        pl.when(has_left)(lambda: side_right(g).wait_recv())
        pl.when(has_right)(lambda: side_left(g).wait_recv())
        edges[g + 1] = jnp.where(even, halo_in[1, g], pltpu.roll(halo_in[0, g], 2, 1))
        if g == 0:
            pl.when(has_up)(lambda: corner_up().start())
        if g == groups - 1:
            pl.when(has_down)(lambda: corner_down().start())

    def corner_up():
        return pltpu.make_async_remote_copy(
            src_ref=edges.at[1], dst_ref=edges.at[groups + 1],
            send_sem=corner_send.at[0], recv_sem=corner_recv.at[0],
            device_id={"gy": my - 1}, device_id_type=MESH,
        )

    def corner_down():
        return pltpu.make_async_remote_copy(
            src_ref=edges.at[groups], dst_ref=edges.at[0],
            send_sem=corner_send.at[1], recv_sem=corner_recv.at[1],
            device_id={"gy": my + 1}, device_id_type=MESH,
        )

    def shift_row(i, sh):
        g = (i - 1 + per) // per
        back = lax.rem(i - 1 + per, per) * 2 * depth
        row_edges = pltpu.roll(edges[g], lax.rem(2 * width - 1 - back, width), 1)
        for z in range(depth):
            tile = xs[i, z + 1]
            edge = row_edges if z == 0 else pltpu.roll(row_edges, width - 2 * z, 1)
            sh[0, z + 1] = jnp.where(lane == 0, edge, pltpu.roll(tile, 1, 1))
            sh[1, z + 1] = jnp.where(lane == width - 1, edge, pltpu.roll(tile, width - 1, 1))

    def window(i, sh, d, z):
        at = pl.ds(z, 4)
        tile = xs[i, at] if d == 1 else sh[d // 2, at]
        return tile.reshape(4 * ch, width)

    def conv_row(i, sh, lo, hi, use):
        for q in range(depth // 4):
            rhs = jnp.concatenate(
                [
                    jnp.concatenate([window(i, sh, d, 4 * q), window(i, sh, d, 4 * q + 2)], axis=1)
                    for d in range(3)
                ],
                axis=0,
            )
            acc = jnp.dot(toep[2 * ch * lo:2 * ch * hi], rhs, preferred_element_type=F32)
            use(q, [acc[2 * ch * a:2 * ch * (a + 1)] for a in range(hi - lo)])

    def lift_out(y, q, done):
        for p in range(2):
            own = xs[y + 1, pl.ds(4 * q + 2 * p + 1, 2)].reshape(2 * ch, width)
            lifted[y, 2 * q + p] = (own.astype(F32) + done[:, p * width:(p + 1) * width]).astype(BF16)

    def lift_row(i, sh):
        def use(q, acc):
            lift_out(i - 2, q, carry_b[q] + acc[2])
            carry_b[q] = carry_a[q] + acc[1]
            carry_a[q] = acc[0]

        conv_row(i, sh, 0, 3, use)

    def modes_of(y, slot):
        tiles = jnp.concatenate(
            [
                jnp.concatenate([lifted[y, PACK * g + j] for j in range(PACK)], axis=1)
                for g in range(quads)
            ],
            axis=0,
        )
        res = jnp.dot(tiles, fwd[...], preferred_element_type=F32).astype(BF16)
        for g in range(quads):
            part[slot * quads + g] = res[2 * ch * g:2 * ch * (g + 1)]

    def mine(c):
        return c * cgroups + core * half + chip * share

    def peer(o):
        return {"gx": 2 * lax.rem(chip + o, chips) + core}

    def tw_copy(c):
        return pltpu.make_async_remote_copy(
            src_ref=part.at[pl.ds(c * cgroups + (1 - core) * half, half)], dst_ref=twin.at[c],
            send_sem=tw_send.at[c], recv_sem=tw_recv.at[c],
            device_id={"gx": me + 1 - 2 * core}, device_id_type=MESH,
        )

    def rs_copy(c, o):
        return pltpu.make_async_remote_copy(
            src_ref=psum.at[c, pl.ds(lax.rem(chip + o, chips) * share, share)], dst_ref=got.at[c, o],
            send_sem=rs_send.at[c, o], recv_sem=rs_recv.at[c, o],
            device_id=peer(o), device_id_type=MESH,
        )

    def ag_copy(c, o):
        at = pl.ds(mine(c), share)
        return pltpu.make_async_remote_copy(
            src_ref=mixed.at[at], dst_ref=mixed.at[at],
            send_sem=ag_send.at[c, o], recv_sem=ag_recv.at[c, o],
            device_id=peer(o), device_id_type=MESH,
        )

    def ag_wait(c, o):
        at = pl.ds(c * cgroups + core * half + lax.rem(chip + chips - o, chips) * share, share)
        pltpu.make_async_remote_copy(
            src_ref=mixed.at[at], dst_ref=mixed.at[at],
            send_sem=ag_send.at[c, o], recv_sem=ag_recv.at[c, o],
            device_id=peer(o), device_id_type=MESH,
        ).wait_recv()

    def fw_copy(c, which):
        at = pl.ds(c * cgroups + which * half, half)
        return pltpu.make_async_remote_copy(
            src_ref=mixed.at[at], dst_ref=mixed.at[at],
            send_sem=fw_send.at[c], recv_sem=fw_recv.at[c],
            device_id={"gx": me + 1 - 2 * core}, device_id_type=MESH,
        )

    def to_twin(c):
        tw_copy(c).start()

    def to_peers(c):
        tw_copy(c).wait_recv()
        own = part[pl.ds(c * cgroups + core * half, half)]
        psum[c] = (own.astype(F32) + twin[c].astype(F32)).astype(BF16)
        pl.loop(1, chips)(lambda o: rs_copy(c, o).start())

    def forward(c):
        pl.loop(1, chips)(lambda o: ag_wait(c, o))
        fw_copy(c, core).start()

    front = lax.broadcasted_iota(jnp.int32, (modes, 2 * ch), 1) < ch

    def mix_chunk(c):
        tsum[...] = psum[c, pl.ds(chip * share, share)].astype(F32)

        @pl.loop(1, chips)
        def _(o):
            rs_copy(c, o).wait_recv()
            tsum[...] += got[c, o].astype(F32)

        for s in range(share):
            flat = tsum[s].T
            for j in range(PACK):
                re = flat[j * j2:j * j2 + modes]
                im = flat[j * j2 + modes:(j + 1) * j2]
                tmix[pl.ds(2 * j * modes, modes)] = jnp.where(front, re, pltpu.roll(im, ch, 1))
                tmix[pl.ds((2 * j + 1) * modes, modes)] = jnp.where(front, pltpu.roll(re, ch, 1), im)
            for k in range(modes):
                at = pl.ds(k, 2 * PACK, stride=modes)
                data = tmix[at, :]
                top = data.astype(BF16).astype(F32)
                lhs = jnp.concatenate([top, data - top], axis=0).astype(BF16)
                both = lax.dot_general(lhs, mixw[k], NT, preferred_element_type=F32)
                tmix[at, :] = both[0:2 * PACK] + both[2 * PACK:4 * PACK]
            lines = []
            for j in range(PACK):
                first = tmix[pl.ds(2 * j * modes, modes)]
                second = tmix[pl.ds((2 * j + 1) * modes, modes)]
                lines.append(jnp.where(front, first, pltpu.roll(second, ch, 1)))
                lines.append(jnp.where(front, pltpu.roll(first, ch, 1), second))
            mixed[mine(c) + s] = jnp.concatenate(lines, axis=0).T.astype(BF16)
        pl.loop(1, chips)(lambda o: ag_copy(c, o).start())

    slope = math.sqrt(2.0 / math.pi)
    low = jnp.asarray(slope, BF16)
    cubic = jnp.asarray(slope * 0.044715, BF16)

    def row_of(slot):
        return lax.rem(slot + 1, rows)

    def blend(slot, to):
        y = row_of(slot)
        spec = mixed[pl.ds(slot * quads, quads)].reshape(quads * 2 * ch, width)
        branch = jnp.dot(
            jnp.concatenate([spec, spec], axis=1), inv[...], preferred_element_type=F32
        )
        for g in range(quads):
            for j in range(PACK):
                p = PACK * g + j
                piece = branch[2 * ch * g:2 * ch * (g + 1), j * width:(j + 1) * width]
                to[p] = (lifted[y, p].astype(F32) + piece).astype(BF16)

    def widen(own, gate):
        for p in range(pairs):
            wide = jnp.concatenate([own[p, 0:ch], own[p, ch:2 * ch]], axis=1)
            h = jnp.dot(up_w[...], wide, preferred_element_type=F32).astype(BF16)
            t = jnp.tanh(h * (low + cubic * (h * h)))
            g = h + h * t
            gate[2 * p] = g[:, :width]
            gate[2 * p + 1] = g[:, width:]

    def narrow(slot, own, gate):
        y = row_of(slot)
        for p in range(pairs):
            g = jnp.concatenate([gate[2 * p], gate[2 * p + 1]], axis=1)
            down = jnp.dot(down_w[...], g, preferred_element_type=F32)
            for z in range(2):
                at = pl.ds(z * ch, ch)
                out[y, p, at] = (
                    own[p, at].astype(F32) + down[:, z * width:(z + 1) * width]
                ).astype(BF16)

    join_edges(0)
    if per < 5:
        join_edges(1)
    shift_row(1, sh_a)
    shift_row(2, sh_b)

    def start_first(q, acc):
        carry_a[q] = acc[0]
        hold[q] = acc[1]

    def start_second(q, acc):
        carry_b[q] = carry_a[q] + acc[1]
        carry_a[q] = acc[0]
        hold[q] += acc[2]

    conv_row(1, sh_a, 0, 2, start_first)
    shift_row(3, sh_a)
    conv_row(2, sh_b, 0, 3, start_second)

    def lift_two(i):
        shift_row(i + 1, sh_b)
        lift_row(i, sh_a)
        shift_row(i + 2, sh_a)
        lift_row(i + 1, sh_b)

    def modes_two(i):
        modes_of(i - 2, i - 3)
        modes_of(i - 1, i - 2)

    def lift_last():
        shift_row(0, sh_b)

        def use_bottom(q, acc):
            lift_out(rows - 1, q, carry_b[q] + acc[0])

        def use_top(q, acc):
            lift_out(0, q, hold[q] + acc[0])

        conv_row(rows + 1, sh_a, 2, 3, use_bottom)
        conv_row(0, sh_b, 0, 1, use_top)

    def last_layers():
        pl.when(has_up)(lambda: row_down().wait_recv())
        pl.when(has_up)(lambda: corner_down().wait_recv())
        pl.when(has_down)(lambda: row_up().wait_recv())
        pl.when(has_down)(lambda: corner_up().wait_recv())

    lifts = rows // 2 - 1
    span = crows // 2
    after = {}

    def book(at, call, rank=-1):
        after.setdefault(at, []).append((rank, call))

    for s in range(1, lifts):
        for g in range(1, groups):
            if (4 + 2 * (s - 1)) // per < g <= (4 + 2 * s) // per:
                book(s - 1, functools.partial(join_edges, g))
    book(lifts - 2, last_layers)
    for c in range(chunks):
        at = min((c + 1) * span - 1, lifts) if c < chunks - 1 else lifts
        due = lifts + c * span
        for call, later in zip((to_twin, to_peers, mix_chunk, forward), LATER[c]):
            place = min(at + later, due)
            rank = 2 * RANKS[call.__name__] + 6 * (call is to_peers and place == at)
            book(place, functools.partial(call, c), rank)

    def then(at):
        calls = after.get(at, [])
        if chunks > 1:
            calls = sorted(calls, key=lambda c: c[0])
        for _, call in calls:
            call()

    def lift_step(s, first, last):
        if not first:
            modes_two(2 * s + 1)
        lift_two(2 * s + 3)
        if last:
            modes_two(2 * s + 3)

    mix_weights()
    if chunks > 1:
        for s in range(lifts):
            lift_step(s, s % span == 0, s % span == span - 1)
            then(s)
        if lifts % span:
            modes_two(2 * lifts + 1)
    else:
        lift_step(0, True, False)
        then(0)

        @pl.loop(1, lifts)
        def _(s):
            lift_step(s, False, False)
            for at in range(1, lifts):
                if at in after:
                    pl.when(s == at)(lambda at=at: then(at))

        modes_two(2 * lifts + 1)
    lift_last()
    modes_of(rows - 1, rows - 2)
    modes_of(0, rows - 1)
    then(lifts)

    def arrive(c):
        fw_copy(c, 1 - core).wait_recv()

    arrive(0)
    blend(0, blend_a)
    widen(blend_a, gate_a)
    blend(1, blend_b)
    then(lifts + 1)

    @pl.loop(1, rows // 2)
    def _(s):
        if chunks > 1:
            pl.when(lax.rem(s, span) == 0)(lambda: arrive(s // span))
        t = 2 * s
        narrow(t - 2, blend_a, gate_a)
        widen(blend_b, gate_b)
        blend(t, blend_a)
        narrow(t - 1, blend_b, gate_b)
        widen(blend_a, gate_a)
        blend(t + 1, blend_b)
        for at in range(1, rows // 2):
            if lifts + 1 + at in after:
                pl.when(s == at)(lambda at=at: then(lifts + 1 + at))

    narrow(rows - 2, blend_a, gate_a)
    widen(blend_b, gate_b)
    narrow(rows - 1, blend_b, gate_b)

    pl.when(has_up)(lambda: row_up().wait_send())
    pl.when(has_down)(lambda: row_down().wait_send())
    pl.when(has_up)(lambda: corner_up().wait_send())
    pl.when(has_down)(lambda: corner_down().wait_send())
    for g in range(groups):
        pl.when(has_left)(lambda g=g: side_left(g).wait_send())
        pl.when(has_right)(lambda g=g: side_right(g).wait_send())
    for c in range(chunks):
        tw_copy(c).wait_send()
        fw_copy(c, core).wait_send()

        @pl.loop(1, chips)
        def _(o):
            rs_copy(c, o).wait_send()
            ag_copy(c, o).wait_send()


def per_device(n, m, field, conv_w, spec_re, spec_im, mlp_in, mlp_out):
    rows, depth, ch, width = field.shape
    modes = spec_re.shape[0]
    pairs = depth // 2
    total_groups = rows * pairs // PACK
    chunks = min(4, total_groups // n)
    share = total_groups // chunks // n
    groups = 2 * rows * depth // width
    dma = pltpu.SemaphoreType.DMA
    hbm = pl.BlockSpec(memory_space=pltpu.HBM)
    tile = (2 * ch, PACK * 2 * modes)
    result = pl.pallas_call(
        functools.partial(kernel, n, m, chunks),
        out_shape=pltpu.VMEM((rows, pairs, 2 * ch, width), BF16),
        in_specs=[hbm] * 6,
        out_specs=pl.BlockSpec(memory_space=pltpu.VMEM),
        scratch_shapes=[
            pltpu.VMEM((rows + 2, depth + 2, ch, width), BF16),
            pltpu.VMEM((2, depth + 2, ch, width), BF16),
            pltpu.VMEM((2, depth + 2, ch, width), BF16),
            pltpu.VMEM((depth // 4, 2 * ch, 2 * width), F32),
            pltpu.VMEM((depth // 4, 2 * ch, 2 * width), F32),
            pltpu.VMEM((depth // 4, 2 * ch, 2 * width), F32),
            pltpu.VMEM((rows, pairs, 2 * ch, width), BF16),
            pltpu.VMEM((groups, ch, width), BF16),
            pltpu.VMEM((2, groups, ch, width), BF16),
            pltpu.VMEM((groups + 2, ch, width), BF16),
            pltpu.VMEM((mlp_in.shape[0], ch), BF16),
            pltpu.VMEM(mlp_out.shape, BF16),
            pltpu.VMEM((6 * ch, 12 * ch), BF16),
            pltpu.VMEM((modes, 2 * ch, 2 * ch), BF16),
            pltpu.VMEM((PACK * width, PACK * 2 * modes), BF16),
            pltpu.VMEM((2 * PACK * 2 * modes, PACK * width), BF16),
            pltpu.VMEM((total_groups,) + tile, BF16),
            pltpu.VMEM((chunks, total_groups // chunks // 2) + tile, BF16),
            pltpu.VMEM((chunks, total_groups // chunks // 2) + tile, BF16),
            pltpu.VMEM((chunks, n // 2, share) + tile, BF16),
            pltpu.VMEM((share,) + tile, F32),
            pltpu.VMEM((PACK * 2 * modes, 2 * ch), F32),
            pltpu.VMEM((total_groups,) + tile, BF16),
            pltpu.VMEM((pairs, 2 * ch, width), BF16),
            pltpu.VMEM((pairs, 2 * ch, width), BF16),
            pltpu.VMEM((depth, mlp_in.shape[0], width), BF16),
            pltpu.VMEM((depth, mlp_in.shape[0], width), BF16),
            pltpu.VMEM(conv_w.shape, BF16),
            pltpu.VMEM(spec_re.shape, F32),
            pltpu.VMEM(spec_im.shape, F32),
            pltpu.VMEM(mlp_in.shape[::-1], BF16),
            pltpu.VMEM(mlp_out.shape, BF16),
            dma((rows,)), dma((5,)),
            dma((2,)), dma((2,)),
            dma((2, groups)), dma((2, groups)),
            dma((2,)), dma((2,)),
            dma((chunks,)), dma((chunks,)),
            dma((chunks, n // 2)), dma((chunks, n // 2)),
            dma((chunks, n // 2)), dma((chunks, n // 2)),
            dma((chunks,)), dma((chunks,)),
        ],
        compiler_params=pltpu.CompilerParams(
            collective_id=0, has_side_effects=True, vmem_limit_bytes=59 << 20
        ),
    )(field, conv_w, spec_re, spec_im, mlp_in.T, mlp_out)
    return result.reshape(rows, depth, ch, width)


def solution(mesh):
    in_specs = (P("gy", None, None, "gx"), P(), P(), P(), P(), P())
    out_specs = P("gy", None, None, "gx")
    return jax.shard_map(
        functools.partial(per_device, mesh.shape["gx"], mesh.shape["gy"]),
        mesh=mesh, in_specs=in_specs, out_specs=out_specs, check_vma=False,
    )
```

```python
import functools
import math

import jax
import jax.numpy as jnp
from jax import lax
from jax.experimental import pallas as pl
from jax.experimental.pallas import tpu as pltpu
from jax.sharding import PartitionSpec as P

F32 = jnp.float32
BF16 = jnp.bfloat16
MESH = pl.DeviceIdType.MESH
NT = (((1,), (1,)), ((), ()))
PACK = 4
LATER = ((0, 1, 4, 6), (0, 1, 4, 5), (0, 1, 3, 5), (0, 0, 2, 5))
RANKS = {"to_twin": 0, "to_peers": 1, "mix_chunk": 2, "forward": 3}


def kernel(
    n, m, chunks, field, conv_w, spec_re, spec_im, mlp_in, mlp_out, out,
    xs, sh_a, sh_b, carry_a, carry_b, hold, lifted, halo_out, halo_in, edges, up_w, down_w, toep, mixw,
    fwd, inv, part, twin, psum, got, tsum, tmix, mixed, blend_a, blend_b, gate_a, gate_b,
    conv_v, re_v, im_v, in_v, out_v,
    load_sem, w_sem, row_send, row_recv, side_send, side_recv, corner_send, corner_recv,
    tw_send, tw_recv, rs_send, rs_recv, ag_send, ag_recv, fw_send, fw_recv,
):
    rows, depth, ch, width = field.shape
    modes = spec_re.shape[0]
    total = n * width
    pairs = depth // 2
    crows = rows // chunks
    quads = pairs // PACK
    cgroups = crows * quads
    share = cgroups // n
    chips = n // 2
    half = cgroups // 2
    per = width // (2 * depth)
    groups = rows // per
    me = lax.axis_index("gx")
    my = lax.axis_index("gy")
    core, chip = lax.rem(me, 2), me // 2
    has_left, has_right = me > 0, me < n - 1
    has_up, has_down = my > 0, my < m - 1

    def load(y):
        return pltpu.make_async_copy(
            field.at[y], xs.at[y + 1, pl.ds(1, depth)], load_sem.at[y]
        )

    weights = [(conv_w, conv_v), (spec_re, re_v), (spec_im, im_v), (mlp_in, in_v), (mlp_out, out_v)]

    def fetch(j):
        return pltpu.make_async_copy(weights[j][0], weights[j][1], w_sem.at[j])

    @pl.loop(0, per)
    def _(y):
        load(y).start()

    fetch(0).start()

    @pl.loop(per, rows)
    def _(y):
        load(y).start()

    for j in range(1, 5):
        fetch(j).start()

    barrier = pltpu.get_barrier_semaphore()

    @pl.loop(1, n)
    def _(o):
        pl.semaphore_signal(
            barrier, inc=1, device_id={"gx": lax.rem(me + o, n)}, device_id_type=MESH
        )

    @pl.when(has_up)
    def _():
        pl.semaphore_signal(barrier, inc=1, device_id={"gy": my - 1}, device_id_type=MESH)

    @pl.when(has_down)
    def _():
        pl.semaphore_signal(barrier, inc=1, device_id={"gy": my + 1}, device_id_type=MESH)

    lane = lax.broadcasted_iota(jnp.int32, (ch, width), 1)

    def pack_edges(g):
        both = jnp.zeros((ch, width), BF16)
        for y in range(per):
            for z in range(depth):
                tile = xs[g * per + y + 1, z + 1]
                to = 2 * (y * depth + z)
                turned = pltpu.roll(tile, to, 1) if to else tile
                hit = (lane == to) | (lane == (to + width - 1) % width)
                both = jnp.where(hit, turned, both)
        halo_out[g] = both

    def side_left(g):
        return pltpu.make_async_remote_copy(
            src_ref=halo_out.at[g], dst_ref=halo_in.at[1, g],
            send_sem=side_send.at[0, g], recv_sem=side_recv.at[1, g],
            device_id={"gx": me - 1}, device_id_type=MESH,
        )

    def side_right(g):
        return pltpu.make_async_remote_copy(
            src_ref=halo_out.at[g], dst_ref=halo_in.at[0, g],
            send_sem=side_send.at[1, g], recv_sem=side_recv.at[0, g],
            device_id={"gx": me + 1}, device_id_type=MESH,
        )

    def row_up():
        return pltpu.make_async_remote_copy(
            src_ref=field.at[0], dst_ref=xs.at[rows + 1, pl.ds(1, depth)],
            send_sem=row_send.at[0], recv_sem=row_recv.at[0],
            device_id={"gy": my - 1}, device_id_type=MESH,
        )

    def row_down():
        return pltpu.make_async_remote_copy(
            src_ref=field.at[rows - 1], dst_ref=xs.at[0, pl.ds(1, depth)],
            send_sem=row_send.at[1], recv_sem=row_recv.at[1],
            device_id={"gy": my + 1}, device_id_type=MESH,
        )

    def send_edges(g):
        @pl.loop(0, per)
        def _(y):
            load(g * per + y).wait()

        pack_edges(g)

    def start_sides(g):
        pl.when(has_left)(lambda: side_left(g).start())
        pl.when(has_right)(lambda: side_right(g).start())

    blank = jnp.zeros((ch, width), BF16)

    @pl.loop(0, rows + 2)
    def _(y):
        xs[y, 0] = blank
        xs[y, depth + 1] = blank

    for sh in (sh_a, sh_b):
        for d in range(2):
            sh[d, 0] = blank
            sh[d, depth + 1] = blank

    @pl.when(jnp.logical_not(has_up))
    def _():
        for z in range(depth):
            xs[0, z + 1] = blank
        edges[0] = blank

    @pl.when(jnp.logical_not(has_down))
    def _():
        for z in range(depth):
            xs[rows + 1, z + 1] = blank
        edges[groups + 1] = blank

    @pl.when(jnp.logical_not(has_left))
    def _():
        for g in range(groups):
            halo_in[0, g] = blank

    @pl.when(jnp.logical_not(has_right))
    def _():
        for g in range(groups):
            halo_in[1, g] = blank

    send_edges(0)
    pl.semaphore_wait(barrier, n - 1 + has_up.astype(jnp.int32) + has_down.astype(jnp.int32))
    start_sides(0)

    @pl.loop(1, groups)
    def _(g):
        send_edges(g)
        start_sides(g)

    pl.when(has_up)(lambda: row_up().start())
    pl.when(has_down)(lambda: row_down().start())

    for j in range(5):
        fetch(j).wait()

    up_w[...] = in_v[...].astype(F32).T.astype(BF16)
    down_w[...] = out_v[...] * jnp.asarray(0.5, BF16)

    square = jnp.zeros((ch, ch), BF16)
    for a in range(3):
        for d in range(3):
            taps = [conv_v[(a * 3 + b) * 3 + d] for b in range(3)]
            cols = pl.ds(d * 4 * ch, 4 * ch)
            toep[pl.ds(2 * a * ch, ch), cols] = jnp.concatenate(taps + [square], axis=1)
            toep[pl.ds((2 * a + 1) * ch, ch), cols] = jnp.concatenate([square] + taps, axis=1)

    def mix_weights():
        for k in range(modes):
            re = re_v[k].astype(BF16)
            im = im_v[k].astype(BF16)
            mixw[k, 0:ch] = jnp.concatenate([re, -im], axis=1)
            mixw[k, ch:2 * ch] = jnp.concatenate([im, re], axis=1)

    j2 = 2 * modes
    places = me * width + lax.broadcasted_iota(jnp.int32, (j2, width), 1)
    order = lax.broadcasted_iota(jnp.int32, (j2, width), 0)
    k_of = lax.rem(order, modes)
    phase = places * k_of + jnp.where(order >= modes, total // 4, 0)
    wave = jnp.cos(lax.rem(phase, total).astype(F32) * (2.0 * math.pi / total))
    scales = jnp.where(k_of == 0, 1.0, 2.0).astype(F32) / total
    table = wave * scales
    high = table.astype(BF16).astype(F32)
    low_part = table - high
    wide_row = lax.broadcasted_iota(jnp.int32, (PACK * j2, width), 0) // j2
    wide_lane = lax.broadcasted_iota(jnp.int32, (width, PACK * j2), 1) // j2
    columns = jnp.concatenate([wave] * PACK, axis=0).T
    tall = [jnp.concatenate([t] * PACK, axis=0) for t in (high, low_part)]
    for j in range(PACK):
        fwd[j * width:(j + 1) * width] = jnp.where(wide_lane == j, columns, 0.0).astype(BF16)
        for h in range(2):
            inv[h * PACK * j2:(h + 1) * PACK * j2, j * width:(j + 1) * width] = jnp.where(
                wide_row == j, tall[h], 0.0
            ).astype(BF16)

    even = lax.rem(lane, 2) == 0
    def join_edges(g):
        pl.when(has_left)(lambda: side_right(g).wait_recv())
        pl.when(has_right)(lambda: side_left(g).wait_recv())
        edges[g + 1] = jnp.where(even, halo_in[1, g], pltpu.roll(halo_in[0, g], 2, 1))
        if g == 0:
            pl.when(has_up)(lambda: corner_up().start())
        if g == groups - 1:
            pl.when(has_down)(lambda: corner_down().start())

    def corner_up():
        return pltpu.make_async_remote_copy(
            src_ref=edges.at[1], dst_ref=edges.at[groups + 1],
            send_sem=corner_send.at[0], recv_sem=corner_recv.at[0],
            device_id={"gy": my - 1}, device_id_type=MESH,
        )

    def corner_down():
        return pltpu.make_async_remote_copy(
            src_ref=edges.at[groups], dst_ref=edges.at[0],
            send_sem=corner_send.at[1], recv_sem=corner_recv.at[1],
            device_id={"gy": my + 1}, device_id_type=MESH,
        )

    def shift_row(i, sh):
        g = (i - 1 + per) // per
        back = lax.rem(i - 1 + per, per) * 2 * depth
        row_edges = pltpu.roll(edges[g], lax.rem(2 * width - 1 - back, width), 1)
        for z in range(depth):
            tile = xs[i, z + 1]
            edge = row_edges if z == 0 else pltpu.roll(row_edges, width - 2 * z, 1)
            sh[0, z + 1] = jnp.where(lane == 0, edge, pltpu.roll(tile, 1, 1))
            sh[1, z + 1] = jnp.where(lane == width - 1, edge, pltpu.roll(tile, width - 1, 1))

    def window(i, sh, d, z):
        at = pl.ds(z, 4)
        tile = xs[i, at] if d == 1 else sh[d // 2, at]
        return tile.reshape(4 * ch, width)

    def conv_row(i, sh, lo, hi, use):
        for q in range(depth // 4):
            rhs = jnp.concatenate(
                [
                    jnp.concatenate([window(i, sh, d, 4 * q), window(i, sh, d, 4 * q + 2)], axis=1)
                    for d in range(3)
                ],
                axis=0,
            )
            acc = jnp.dot(toep[2 * ch * lo:2 * ch * hi], rhs, preferred_element_type=F32)
            use(q, [acc[2 * ch * a:2 * ch * (a + 1)] for a in range(hi - lo)])

    def lift_out(y, q, done):
        for p in range(2):
            own = xs[y + 1, pl.ds(4 * q + 2 * p + 1, 2)].reshape(2 * ch, width)
            lifted[y, 2 * q + p] = (own.astype(F32) + done[:, p * width:(p + 1) * width]).astype(BF16)

    def lift_row(i, sh):
        def use(q, acc):
            lift_out(i - 2, q, carry_b[q] + acc[2])
            carry_b[q] = carry_a[q] + acc[1]
            carry_a[q] = acc[0]

        conv_row(i, sh, 0, 3, use)

    def modes_of(y, slot):
        tiles = jnp.concatenate(
            [
                jnp.concatenate([lifted[y, PACK * g + j] for j in range(PACK)], axis=1)
                for g in range(quads)
            ],
            axis=0,
        )
        res = jnp.dot(tiles, fwd[...], preferred_element_type=F32).astype(BF16)
        for g in range(quads):
            part[slot * quads + g] = res[2 * ch * g:2 * ch * (g + 1)]

    def mine(c):
        return c * cgroups + core * half + chip * share

    def peer(o):
        return {"gx": 2 * lax.rem(chip + o, chips) + core}

    def tw_copy(c):
        return pltpu.make_async_remote_copy(
            src_ref=part.at[pl.ds(c * cgroups + (1 - core) * half, half)], dst_ref=twin.at[c],
            send_sem=tw_send.at[c], recv_sem=tw_recv.at[c],
            device_id={"gx": me + 1 - 2 * core}, device_id_type=MESH,
        )

    def rs_copy(c, o):
        return pltpu.make_async_remote_copy(
            src_ref=psum.at[c, pl.ds(lax.rem(chip + o, chips) * share, share)], dst_ref=got.at[c, o],
            send_sem=rs_send.at[c, o], recv_sem=rs_recv.at[c, o],
            device_id=peer(o), device_id_type=MESH,
        )

    def ag_copy(c, o):
        at = pl.ds(mine(c), share)
        return pltpu.make_async_remote_copy(
            src_ref=mixed.at[at], dst_ref=mixed.at[at],
            send_sem=ag_send.at[c, o], recv_sem=ag_recv.at[c, o],
            device_id=peer(o), device_id_type=MESH,
        )

    def ag_wait(c, o):
        at = pl.ds(c * cgroups + core * half + lax.rem(chip + chips - o, chips) * share, share)
        pltpu.make_async_remote_copy(
            src_ref=mixed.at[at], dst_ref=mixed.at[at],
            send_sem=ag_send.at[c, o], recv_sem=ag_recv.at[c, o],
            device_id=peer(o), device_id_type=MESH,
        ).wait_recv()

    def fw_copy(c, which):
        at = pl.ds(c * cgroups + which * half, half)
        return pltpu.make_async_remote_copy(
            src_ref=mixed.at[at], dst_ref=mixed.at[at],
            send_sem=fw_send.at[c], recv_sem=fw_recv.at[c],
            device_id={"gx": me + 1 - 2 * core}, device_id_type=MESH,
        )

    def to_twin(c):
        tw_copy(c).start()

    def to_peers(c):
        tw_copy(c).wait_recv()
        own = part[pl.ds(c * cgroups + core * half, half)]
        psum[c] = (own.astype(F32) + twin[c].astype(F32)).astype(BF16)
        pl.loop(1, chips)(lambda o: rs_copy(c, o).start())

    def forward(c):
        pl.loop(1, chips)(lambda o: ag_wait(c, o))
        fw_copy(c, core).start()

    front = lax.broadcasted_iota(jnp.int32, (modes, 2 * ch), 1) < ch

    def mix_chunk(c):
        tsum[...] = psum[c, pl.ds(chip * share, share)].astype(F32)

        @pl.loop(1, chips)
        def _(o):
            rs_copy(c, o).wait_recv()
            tsum[...] += got[c, o].astype(F32)

        for s in range(share):
            flat = tsum[s].T
            for j in range(PACK):
                re = flat[j * j2:j * j2 + modes]
                im = flat[j * j2 + modes:(j + 1) * j2]
                tmix[pl.ds(2 * j * modes, modes)] = jnp.where(front, re, pltpu.roll(im, ch, 1))
                tmix[pl.ds((2 * j + 1) * modes, modes)] = jnp.where(front, pltpu.roll(re, ch, 1), im)
            for k in range(modes):
                at = pl.ds(k, 2 * PACK, stride=modes)
                data = tmix[at, :]
                top = data.astype(BF16).astype(F32)
                lhs = jnp.concatenate([top, data - top], axis=0).astype(BF16)
                both = lax.dot_general(lhs, mixw[k], NT, preferred_element_type=F32)
                tmix[at, :] = both[0:2 * PACK] + both[2 * PACK:4 * PACK]
            lines = []
            for j in range(PACK):
                first = tmix[pl.ds(2 * j * modes, modes)]
                second = tmix[pl.ds((2 * j + 1) * modes, modes)]
                lines.append(jnp.where(front, first, pltpu.roll(second, ch, 1)))
                lines.append(jnp.where(front, pltpu.roll(first, ch, 1), second))
            mixed[mine(c) + s] = jnp.concatenate(lines, axis=0).T.astype(BF16)
        pl.loop(1, chips)(lambda o: ag_copy(c, o).start())

    slope = math.sqrt(2.0 / math.pi)
    low = jnp.asarray(slope, BF16)
    cubic = jnp.asarray(slope * 0.044715, BF16)

    def row_of(slot):
        return lax.rem(slot + 1, rows)

    def blend(slot, to):
        y = row_of(slot)
        spec = mixed[pl.ds(slot * quads, quads)].reshape(quads * 2 * ch, width)
        branch = jnp.dot(
            jnp.concatenate([spec, spec], axis=1), inv[...], preferred_element_type=F32
        )
        for g in range(quads):
            for j in range(PACK):
                p = PACK * g + j
                piece = branch[2 * ch * g:2 * ch * (g + 1), j * width:(j + 1) * width]
                to[p] = (lifted[y, p].astype(F32) + piece).astype(BF16)

    def widen(own, gate, span=None):
        for p in range(pairs) if span is None else span:
            wide = jnp.concatenate([own[p, 0:ch], own[p, ch:2 * ch]], axis=1)
            h = jnp.dot(up_w[...], wide, preferred_element_type=F32).astype(BF16)
            t = jnp.tanh(h * (low + cubic * (h * h)))
            gate[p] = h + h * t

    def narrow(slot, own, gate, span=None):
        y = row_of(slot)
        for p in range(pairs) if span is None else span:
            down = jnp.dot(down_w[...], gate[p], preferred_element_type=F32)
            for z in range(2):
                at = pl.ds(z * ch, ch)
                out[y, p, at] = (
                    own[p, at].astype(F32) + down[:, z * width:(z + 1) * width]
                ).astype(BF16)

    join_edges(0)
    if per < 5:
        join_edges(1)
    shift_row(1, sh_a)
    shift_row(2, sh_b)

    def start_first(q, acc):
        carry_a[q] = acc[0]
        hold[q] = acc[1]

    def start_second(q, acc):
        carry_b[q] = carry_a[q] + acc[1]
        carry_a[q] = acc[0]
        hold[q] += acc[2]

    conv_row(1, sh_a, 0, 2, start_first)
    shift_row(3, sh_a)
    conv_row(2, sh_b, 0, 3, start_second)

    def lift_two(i):
        shift_row(i + 1, sh_b)
        lift_row(i, sh_a)
        shift_row(i + 2, sh_a)
        lift_row(i + 1, sh_b)

    def modes_two(i):
        modes_of(i - 2, i - 3)
        modes_of(i - 1, i - 2)

    def lift_last():
        shift_row(0, sh_b)

        def use_bottom(q, acc):
            lift_out(rows - 1, q, carry_b[q] + acc[0])

        def use_top(q, acc):
            lift_out(0, q, hold[q] + acc[0])

        conv_row(rows + 1, sh_a, 2, 3, use_bottom)
        conv_row(0, sh_b, 0, 1, use_top)

    def last_layers():
        pl.when(has_up)(lambda: row_down().wait_recv())
        pl.when(has_up)(lambda: corner_down().wait_recv())
        pl.when(has_down)(lambda: row_up().wait_recv())
        pl.when(has_down)(lambda: corner_up().wait_recv())

    lifts = rows // 2 - 1
    span = crows // 2
    after = {}

    def book(at, call, rank=-1):
        after.setdefault(at, []).append((rank, call))

    for s in range(1, lifts):
        for g in range(1, groups):
            if (4 + 2 * (s - 1)) // per < g <= (4 + 2 * s) // per:
                book(s - 1, functools.partial(join_edges, g))
    book(lifts - 2, last_layers)
    for c in range(chunks):
        at = min((c + 1) * span - 1, lifts) if c < chunks - 1 else lifts
        due = lifts + c * span
        for call, later in zip((to_twin, to_peers, mix_chunk, forward), LATER[c]):
            place = min(at + later, due)
            rank = 2 * RANKS[call.__name__] + 6 * (call is to_peers and place == at)
            book(place, functools.partial(call, c), rank)

    def then(at):
        calls = after.get(at, [])
        if chunks > 1:
            calls = sorted(calls, key=lambda c: c[0])
        for _, call in calls:
            call()

    def lift_step(s, first, last):
        if not first:
            modes_two(2 * s + 1)
        lift_two(2 * s + 3)
        if last:
            modes_two(2 * s + 3)

    mix_weights()
    if chunks > 1:
        for s in range(lifts):
            lift_step(s, s % span == 0, s % span == span - 1)
            then(s)
        if lifts % span:
            modes_two(2 * lifts + 1)
    else:
        lift_step(0, True, False)
        then(0)

        @pl.loop(1, lifts)
        def _(s):
            lift_step(s, False, False)
            for at in range(1, lifts):
                if at in after:
                    pl.when(s == at)(lambda at=at: then(at))

        modes_two(2 * lifts + 1)
    lift_last()
    modes_of(rows - 1, rows - 2)
    modes_of(0, rows - 1)
    then(lifts)

    def arrive(c):
        fw_copy(c, 1 - core).wait_recv()

    arrive(0)
    blend(0, blend_a)
    widen(blend_a, gate_a)
    blend(1, blend_b)
    then(lifts + 1)

    @pl.loop(1, rows // 2)
    def _(s):
        if chunks > 1:
            pl.when(lax.rem(s, span) == 0)(lambda: arrive(s // span))
        t = 2 * s
        for p in range(pairs):
            widen(blend_b, gate_b, [p])
            narrow(t - 2, blend_a, gate_a, [p])
        blend(t, blend_a)
        for p in range(pairs):
            widen(blend_a, gate_a, [p])
            narrow(t - 1, blend_b, gate_b, [p])
        blend(t + 1, blend_b)
        for at in range(1, rows // 2):
            if lifts + 1 + at in after:
                pl.when(s == at)(lambda at=at: then(lifts + 1 + at))

    narrow(rows - 2, blend_a, gate_a)
    widen(blend_b, gate_b)
    narrow(rows - 1, blend_b, gate_b)

    pl.when(has_up)(lambda: row_up().wait_send())
    pl.when(has_down)(lambda: row_down().wait_send())
    pl.when(has_up)(lambda: corner_up().wait_send())
    pl.when(has_down)(lambda: corner_down().wait_send())
    for g in range(groups):
        pl.when(has_left)(lambda g=g: side_left(g).wait_send())
        pl.when(has_right)(lambda g=g: side_right(g).wait_send())
    for c in range(chunks):
        tw_copy(c).wait_send()
        fw_copy(c, core).wait_send()

        @pl.loop(1, chips)
        def _(o):
            rs_copy(c, o).wait_send()
            ag_copy(c, o).wait_send()


def per_device(n, m, field, conv_w, spec_re, spec_im, mlp_in, mlp_out):
    rows, depth, ch, width = field.shape
    modes = spec_re.shape[0]
    pairs = depth // 2
    total_groups = rows * pairs // PACK
    chunks = min(4, total_groups // n)
    share = total_groups // chunks // n
    groups = 2 * rows * depth // width
    dma = pltpu.SemaphoreType.DMA
    hbm = pl.BlockSpec(memory_space=pltpu.HBM)
    tile = (2 * ch, PACK * 2 * modes)
    result = pl.pallas_call(
        functools.partial(kernel, n, m, chunks),
        out_shape=pltpu.VMEM((rows, pairs, 2 * ch, width), BF16),
        in_specs=[hbm] * 6,
        out_specs=pl.BlockSpec(memory_space=pltpu.VMEM),
        scratch_shapes=[
            pltpu.VMEM((rows + 2, depth + 2, ch, width), BF16),
            pltpu.VMEM((2, depth + 2, ch, width), BF16),
            pltpu.VMEM((2, depth + 2, ch, width), BF16),
            pltpu.VMEM((depth // 4, 2 * ch, 2 * width), F32),
            pltpu.VMEM((depth // 4, 2 * ch, 2 * width), F32),
            pltpu.VMEM((depth // 4, 2 * ch, 2 * width), F32),
            pltpu.VMEM((rows, pairs, 2 * ch, width), BF16),
            pltpu.VMEM((groups, ch, width), BF16),
            pltpu.VMEM((2, groups, ch, width), BF16),
            pltpu.VMEM((groups + 2, ch, width), BF16),
            pltpu.VMEM((mlp_in.shape[0], ch), BF16),
            pltpu.VMEM(mlp_out.shape, BF16),
            pltpu.VMEM((6 * ch, 12 * ch), BF16),
            pltpu.VMEM((modes, 2 * ch, 2 * ch), BF16),
            pltpu.VMEM((PACK * width, PACK * 2 * modes), BF16),
            pltpu.VMEM((2 * PACK * 2 * modes, PACK * width), BF16),
            pltpu.VMEM((total_groups,) + tile, BF16),
            pltpu.VMEM((chunks, total_groups // chunks // 2) + tile, BF16),
            pltpu.VMEM((chunks, total_groups // chunks // 2) + tile, BF16),
            pltpu.VMEM((chunks, n // 2, share) + tile, BF16),
            pltpu.VMEM((share,) + tile, F32),
            pltpu.VMEM((PACK * 2 * modes, 2 * ch), F32),
            pltpu.VMEM((total_groups,) + tile, BF16),
            pltpu.VMEM((pairs, 2 * ch, width), BF16),
            pltpu.VMEM((pairs, 2 * ch, width), BF16),
            pltpu.VMEM((pairs, mlp_in.shape[0], 2 * width), BF16),
            pltpu.VMEM((pairs, mlp_in.shape[0], 2 * width), BF16),
            pltpu.VMEM(conv_w.shape, BF16),
            pltpu.VMEM(spec_re.shape, F32),
            pltpu.VMEM(spec_im.shape, F32),
            pltpu.VMEM(mlp_in.shape[::-1], BF16),
            pltpu.VMEM(mlp_out.shape, BF16),
            dma((rows,)), dma((5,)),
            dma((2,)), dma((2,)),
            dma((2, groups)), dma((2, groups)),
            dma((2,)), dma((2,)),
            dma((chunks,)), dma((chunks,)),
            dma((chunks, n // 2)), dma((chunks, n // 2)),
            dma((chunks, n // 2)), dma((chunks, n // 2)),
            dma((chunks,)), dma((chunks,)),
        ],
        compiler_params=pltpu.CompilerParams(
            collective_id=0, has_side_effects=True, vmem_limit_bytes=59 << 20
        ),
    )(field, conv_w, spec_re, spec_im, mlp_in.T, mlp_out)
    return result.reshape(rows, depth, ch, width)


def solution(mesh):
    in_specs = (P("gy", None, None, "gx"), P(), P(), P(), P(), P())
    out_specs = P("gy", None, None, "gx")
    return jax.shard_map(
        functools.partial(per_device, mesh.shape["gx"], mesh.shape["gy"]),
        mesh=mesh, in_specs=in_specs, out_specs=out_specs, check_vma=False,
    )
```

```python
import functools
import math

import jax
import jax.numpy as jnp
from jax import lax
from jax.experimental import pallas as pl
from jax.experimental.pallas import tpu as pltpu
from jax.sharding import PartitionSpec as P

F32 = jnp.float32
BF16 = jnp.bfloat16
MESH = pl.DeviceIdType.MESH
NT = (((1,), (1,)), ((), ()))
PACK = 4
LATER = ((0, 1, 3, 6), (0, 1, 4, 5), (0, 1, 3, 5), (0, 0, 2, 5))
RANKS = {"to_twin": 0, "to_peers": 1, "mix_chunk": 2, "forward": 3}


def kernel(
    n, m, chunks, field, conv_w, spec_re, spec_im, mlp_in, mlp_out, out,
    xs, sh_a, sh_b, carry_a, carry_b, hold, lifted, halo_out, halo_in, edges, up_w, down_w, toep, mixw,
    fwd, inv, part, twin, psum, got, tsum, tmix, mixed, blend_a, blend_b, gate_a, gate_b,
    conv_v, re_v, im_v, in_v, out_v,
    load_sem, w_sem, row_send, row_recv, side_send, side_recv, corner_send, corner_recv,
    tw_send, tw_recv, rs_send, rs_recv, ag_send, ag_recv, fw_send, fw_recv,
):
    rows, depth, ch, width = field.shape
    modes = spec_re.shape[0]
    total = n * width
    pairs = depth // 2
    crows = rows // chunks
    quads = pairs // PACK
    cgroups = crows * quads
    share = cgroups // n
    chips = n // 2
    half = cgroups // 2
    per = width // (2 * depth)
    groups = rows // per
    me = lax.axis_index("gx")
    my = lax.axis_index("gy")
    core, chip = lax.rem(me, 2), me // 2
    has_left, has_right = me > 0, me < n - 1
    has_up, has_down = my > 0, my < m - 1

    def load(y):
        return pltpu.make_async_copy(
            field.at[y], xs.at[y + 1, pl.ds(1, depth)], load_sem.at[y]
        )

    weights = [(conv_w, conv_v), (spec_re, re_v), (spec_im, im_v), (mlp_in, in_v), (mlp_out, out_v)]

    def fetch(j):
        return pltpu.make_async_copy(weights[j][0], weights[j][1], w_sem.at[j])

    @pl.loop(0, per)
    def _(y):
        load(y).start()

    fetch(0).start()

    @pl.loop(per, rows)
    def _(y):
        load(y).start()

    for j in range(1, 5):
        fetch(j).start()

    barrier = pltpu.get_barrier_semaphore()

    @pl.loop(1, n)
    def _(o):
        pl.semaphore_signal(
            barrier, inc=1, device_id={"gx": lax.rem(me + o, n)}, device_id_type=MESH
        )

    @pl.when(has_up)
    def _():
        pl.semaphore_signal(barrier, inc=1, device_id={"gy": my - 1}, device_id_type=MESH)

    @pl.when(has_down)
    def _():
        pl.semaphore_signal(barrier, inc=1, device_id={"gy": my + 1}, device_id_type=MESH)

    lane = lax.broadcasted_iota(jnp.int32, (ch, width), 1)

    def pack_edges(g):
        both = jnp.zeros((ch, width), BF16)
        for y in range(per):
            for z in range(depth):
                tile = xs[g * per + y + 1, z + 1]
                to = 2 * (y * depth + z)
                turned = pltpu.roll(tile, to, 1) if to else tile
                hit = (lane == to) | (lane == (to + width - 1) % width)
                both = jnp.where(hit, turned, both)
        halo_out[g] = both

    def side_left(g):
        return pltpu.make_async_remote_copy(
            src_ref=halo_out.at[g], dst_ref=halo_in.at[1, g],
            send_sem=side_send.at[0, g], recv_sem=side_recv.at[1, g],
            device_id={"gx": me - 1}, device_id_type=MESH,
        )

    def side_right(g):
        return pltpu.make_async_remote_copy(
            src_ref=halo_out.at[g], dst_ref=halo_in.at[0, g],
            send_sem=side_send.at[1, g], recv_sem=side_recv.at[0, g],
            device_id={"gx": me + 1}, device_id_type=MESH,
        )

    def row_up():
        return pltpu.make_async_remote_copy(
            src_ref=field.at[0], dst_ref=xs.at[rows + 1, pl.ds(1, depth)],
            send_sem=row_send.at[0], recv_sem=row_recv.at[0],
            device_id={"gy": my - 1}, device_id_type=MESH,
        )

    def row_down():
        return pltpu.make_async_remote_copy(
            src_ref=field.at[rows - 1], dst_ref=xs.at[0, pl.ds(1, depth)],
            send_sem=row_send.at[1], recv_sem=row_recv.at[1],
            device_id={"gy": my + 1}, device_id_type=MESH,
        )

    def send_edges(g):
        @pl.loop(0, per)
        def _(y):
            load(g * per + y).wait()

        pack_edges(g)

    def start_sides(g):
        pl.when(has_left)(lambda: side_left(g).start())
        pl.when(has_right)(lambda: side_right(g).start())

    blank = jnp.zeros((ch, width), BF16)

    @pl.loop(0, rows + 2)
    def _(y):
        xs[y, 0] = blank
        xs[y, depth + 1] = blank

    for sh in (sh_a, sh_b):
        for d in range(2):
            sh[d, 0] = blank
            sh[d, depth + 1] = blank

    @pl.when(jnp.logical_not(has_up))
    def _():
        for z in range(depth):
            xs[0, z + 1] = blank
        edges[0] = blank

    @pl.when(jnp.logical_not(has_down))
    def _():
        for z in range(depth):
            xs[rows + 1, z + 1] = blank
        edges[groups + 1] = blank

    @pl.when(jnp.logical_not(has_left))
    def _():
        for g in range(groups):
            halo_in[0, g] = blank

    @pl.when(jnp.logical_not(has_right))
    def _():
        for g in range(groups):
            halo_in[1, g] = blank

    send_edges(0)
    pl.semaphore_wait(barrier, n - 1 + has_up.astype(jnp.int32) + has_down.astype(jnp.int32))
    start_sides(0)

    @pl.loop(1, groups)
    def _(g):
        send_edges(g)
        start_sides(g)

    pl.when(has_up)(lambda: row_up().start())
    pl.when(has_down)(lambda: row_down().start())

    for j in range(5):
        fetch(j).wait()

    up_w[...] = in_v[...].astype(F32).T.astype(BF16)
    down_w[...] = out_v[...] * jnp.asarray(0.5, BF16)

    square = jnp.zeros((ch, ch), BF16)
    for a in range(3):
        for d in range(3):
            taps = [conv_v[(a * 3 + b) * 3 + d] for b in range(3)]
            cols = pl.ds(d * 4 * ch, 4 * ch)
            toep[pl.ds(2 * a * ch, ch), cols] = jnp.concatenate(taps + [square], axis=1)
            toep[pl.ds((2 * a + 1) * ch, ch), cols] = jnp.concatenate([square] + taps, axis=1)

    def mix_weights():
        for k in range(modes):
            re = re_v[k].astype(BF16)
            im = im_v[k].astype(BF16)
            mixw[k, 0:ch] = jnp.concatenate([re, -im], axis=1)
            mixw[k, ch:2 * ch] = jnp.concatenate([im, re], axis=1)

    j2 = 2 * modes
    places = me * width + lax.broadcasted_iota(jnp.int32, (j2, width), 1)
    order = lax.broadcasted_iota(jnp.int32, (j2, width), 0)
    k_of = lax.rem(order, modes)
    phase = places * k_of + jnp.where(order >= modes, total // 4, 0)
    wave = jnp.cos(lax.rem(phase, total).astype(F32) * (2.0 * math.pi / total))
    scales = jnp.where(k_of == 0, 1.0, 2.0).astype(F32) / total
    table = wave * scales
    high = table.astype(BF16).astype(F32)
    low_part = table - high
    wide_row = lax.broadcasted_iota(jnp.int32, (PACK * j2, width), 0) // j2
    wide_lane = lax.broadcasted_iota(jnp.int32, (width, PACK * j2), 1) // j2
    columns = jnp.concatenate([wave] * PACK, axis=0).T
    tall = [jnp.concatenate([t] * PACK, axis=0) for t in (high, low_part)]
    for j in range(PACK):
        fwd[j * width:(j + 1) * width] = jnp.where(wide_lane == j, columns, 0.0).astype(BF16)
        for h in range(2):
            inv[h * PACK * j2:(h + 1) * PACK * j2, j * width:(j + 1) * width] = jnp.where(
                wide_row == j, tall[h], 0.0
            ).astype(BF16)

    even = lax.rem(lane, 2) == 0
    def join_edges(g):
        pl.when(has_left)(lambda: side_right(g).wait_recv())
        pl.when(has_right)(lambda: side_left(g).wait_recv())
        edges[g + 1] = jnp.where(even, halo_in[1, g], pltpu.roll(halo_in[0, g], 2, 1))
        if g == 0:
            pl.when(has_up)(lambda: corner_up().start())
        if g == groups - 1:
            pl.when(has_down)(lambda: corner_down().start())

    def corner_up():
        return pltpu.make_async_remote_copy(
            src_ref=edges.at[1], dst_ref=edges.at[groups + 1],
            send_sem=corner_send.at[0], recv_sem=corner_recv.at[0],
            device_id={"gy": my - 1}, device_id_type=MESH,
        )

    def corner_down():
        return pltpu.make_async_remote_copy(
            src_ref=edges.at[groups], dst_ref=edges.at[0],
            send_sem=corner_send.at[1], recv_sem=corner_recv.at[1],
            device_id={"gy": my + 1}, device_id_type=MESH,
        )

    def shift_row(i, sh):
        g = (i - 1 + per) // per
        back = lax.rem(i - 1 + per, per) * 2 * depth
        row_edges = pltpu.roll(edges[g], lax.rem(2 * width - 1 - back, width), 1)
        for z in range(depth):
            tile = xs[i, z + 1]
            edge = row_edges if z == 0 else pltpu.roll(row_edges, width - 2 * z, 1)
            sh[0, z + 1] = jnp.where(lane == 0, edge, pltpu.roll(tile, 1, 1))
            sh[1, z + 1] = jnp.where(lane == width - 1, edge, pltpu.roll(tile, width - 1, 1))

    def window(i, sh, d, z):
        at = pl.ds(z, 4)
        tile = xs[i, at] if d == 1 else sh[d // 2, at]
        return tile.reshape(4 * ch, width)

    def conv_row(i, sh, lo, hi, use):
        for q in range(depth // 4):
            rhs = jnp.concatenate(
                [
                    jnp.concatenate([window(i, sh, d, 4 * q), window(i, sh, d, 4 * q + 2)], axis=1)
                    for d in range(3)
                ],
                axis=0,
            )
            acc = jnp.dot(toep[2 * ch * lo:2 * ch * hi], rhs, preferred_element_type=F32)
            use(q, [acc[2 * ch * a:2 * ch * (a + 1)] for a in range(hi - lo)])

    def lift_out(y, q, done):
        for p in range(2):
            own = xs[y + 1, pl.ds(4 * q + 2 * p + 1, 2)].reshape(2 * ch, width)
            lifted[y, 2 * q + p] = (own.astype(F32) + done[:, p * width:(p + 1) * width]).astype(BF16)

    def lift_row(i, sh):
        def use(q, acc):
            lift_out(i - 2, q, carry_b[q] + acc[2])
            carry_b[q] = carry_a[q] + acc[1]
            carry_a[q] = acc[0]

        conv_row(i, sh, 0, 3, use)

    def modes_of(y, slot):
        tiles = jnp.concatenate(
            [
                jnp.concatenate([lifted[y, PACK * g + j] for j in range(PACK)], axis=1)
                for g in range(quads)
            ],
            axis=0,
        )
        res = jnp.dot(tiles, fwd[...], preferred_element_type=F32).astype(BF16)
        for g in range(quads):
            part[slot * quads + g] = res[2 * ch * g:2 * ch * (g + 1)]

    def mine(c):
        return c * cgroups + core * half + chip * share

    def peer(o):
        return {"gx": 2 * lax.rem(chip + o, chips) + core}

    def tw_copy(c):
        return pltpu.make_async_remote_copy(
            src_ref=part.at[pl.ds(c * cgroups + (1 - core) * half, half)], dst_ref=twin.at[c],
            send_sem=tw_send.at[c], recv_sem=tw_recv.at[c],
            device_id={"gx": me + 1 - 2 * core}, device_id_type=MESH,
        )

    def rs_copy(c, o):
        return pltpu.make_async_remote_copy(
            src_ref=psum.at[c, pl.ds(lax.rem(chip + o, chips) * share, share)], dst_ref=got.at[c, o],
            send_sem=rs_send.at[c, o], recv_sem=rs_recv.at[c, o],
            device_id=peer(o), device_id_type=MESH,
        )

    def ag_copy(c, o):
        at = pl.ds(mine(c), share)
        return pltpu.make_async_remote_copy(
            src_ref=mixed.at[at], dst_ref=mixed.at[at],
            send_sem=ag_send.at[c, o], recv_sem=ag_recv.at[c, o],
            device_id=peer(o), device_id_type=MESH,
        )

    def ag_wait(c, o):
        at = pl.ds(c * cgroups + core * half + lax.rem(chip + chips - o, chips) * share, share)
        pltpu.make_async_remote_copy(
            src_ref=mixed.at[at], dst_ref=mixed.at[at],
            send_sem=ag_send.at[c, o], recv_sem=ag_recv.at[c, o],
            device_id=peer(o), device_id_type=MESH,
        ).wait_recv()

    def fw_copy(c, which):
        at = pl.ds(c * cgroups + which * half, half)
        return pltpu.make_async_remote_copy(
            src_ref=mixed.at[at], dst_ref=mixed.at[at],
            send_sem=fw_send.at[c], recv_sem=fw_recv.at[c],
            device_id={"gx": me + 1 - 2 * core}, device_id_type=MESH,
        )

    def to_twin(c):
        tw_copy(c).start()

    def to_peers(c):
        tw_copy(c).wait_recv()
        own = part[pl.ds(c * cgroups + core * half, half)]
        psum[c] = (own.astype(F32) + twin[c].astype(F32)).astype(BF16)
        pl.loop(1, chips)(lambda o: rs_copy(c, o).start())

    def forward(c):
        pl.loop(1, chips)(lambda o: ag_wait(c, o))
        fw_copy(c, core).start()

    front = lax.broadcasted_iota(jnp.int32, (modes, 2 * ch), 1) < ch

    def mix_chunk(c):
        tsum[...] = psum[c, pl.ds(chip * share, share)].astype(F32)

        @pl.loop(1, chips)
        def _(o):
            rs_copy(c, o).wait_recv()
            tsum[...] += got[c, o].astype(F32)

        for s in range(share):
            flat = tsum[s].T
            for j in range(PACK):
                re = flat[j * j2:j * j2 + modes]
                im = flat[j * j2 + modes:(j + 1) * j2]
                tmix[pl.ds(2 * j * modes, modes)] = jnp.where(front, re, pltpu.roll(im, ch, 1))
                tmix[pl.ds((2 * j + 1) * modes, modes)] = jnp.where(front, pltpu.roll(re, ch, 1), im)
            for k in range(modes):
                at = pl.ds(k, 2 * PACK, stride=modes)
                data = tmix[at, :]
                top = data.astype(BF16).astype(F32)
                lhs = jnp.concatenate([top, data - top], axis=0).astype(BF16)
                both = lax.dot_general(lhs, mixw[k], NT, preferred_element_type=F32)
                tmix[at, :] = both[0:2 * PACK] + both[2 * PACK:4 * PACK]
            lines = []
            for j in range(PACK):
                first = tmix[pl.ds(2 * j * modes, modes)]
                second = tmix[pl.ds((2 * j + 1) * modes, modes)]
                lines.append(jnp.where(front, first, pltpu.roll(second, ch, 1)))
                lines.append(jnp.where(front, pltpu.roll(first, ch, 1), second))
            mixed[mine(c) + s] = jnp.concatenate(lines, axis=0).T.astype(BF16)
        pl.loop(1, chips)(lambda o: ag_copy(c, o).start())

    slope = math.sqrt(2.0 / math.pi)
    low = jnp.asarray(slope, BF16)
    cubic = jnp.asarray(slope * 0.044715, BF16)

    def row_of(slot):
        return lax.rem(slot + 1, rows)

    def blend(slot, to):
        y = row_of(slot)
        spec = mixed[pl.ds(slot * quads, quads)].reshape(quads * 2 * ch, width)
        branch = jnp.dot(
            jnp.concatenate([spec, spec], axis=1), inv[...], preferred_element_type=F32
        )
        for g in range(quads):
            for j in range(PACK):
                p = PACK * g + j
                piece = branch[2 * ch * g:2 * ch * (g + 1), j * width:(j + 1) * width]
                to[p] = (lifted[y, p].astype(F32) + piece).astype(BF16)

    def widen(own, gate, span=None):
        for p in range(pairs) if span is None else span:
            wide = jnp.concatenate([own[p, 0:ch], own[p, ch:2 * ch]], axis=1)
            h = jnp.dot(up_w[...], wide, preferred_element_type=F32).astype(BF16)
            t = jnp.tanh(h * (low + cubic * (h * h)))
            gate[p] = h + h * t

    def narrow(slot, own, gate, span=None):
        y = row_of(slot)
        for p in range(pairs) if span is None else span:
            down = jnp.dot(down_w[...], gate[p], preferred_element_type=F32)
            for z in range(2):
                at = pl.ds(z * ch, ch)
                out[y, p, at] = (
                    own[p, at].astype(F32) + down[:, z * width:(z + 1) * width]
                ).astype(BF16)

    join_edges(0)
    if per < 5:
        join_edges(1)
    shift_row(1, sh_a)
    shift_row(2, sh_b)

    def start_first(q, acc):
        carry_a[q] = acc[0]
        hold[q] = acc[1]

    def start_second(q, acc):
        carry_b[q] = carry_a[q] + acc[1]
        carry_a[q] = acc[0]
        hold[q] += acc[2]

    conv_row(1, sh_a, 0, 2, start_first)
    shift_row(3, sh_a)
    conv_row(2, sh_b, 0, 3, start_second)

    def lift_two(i):
        shift_row(i + 1, sh_b)
        lift_row(i, sh_a)
        shift_row(i + 2, sh_a)
        lift_row(i + 1, sh_b)

    def modes_two(i):
        modes_of(i - 2, i - 3)
        modes_of(i - 1, i - 2)

    def lift_last():
        shift_row(0, sh_b)

        def use_bottom(q, acc):
            lift_out(rows - 1, q, carry_b[q] + acc[0])

        def use_top(q, acc):
            lift_out(0, q, hold[q] + acc[0])

        conv_row(rows + 1, sh_a, 2, 3, use_bottom)
        conv_row(0, sh_b, 0, 1, use_top)

    def last_layers():
        pl.when(has_up)(lambda: row_down().wait_recv())
        pl.when(has_up)(lambda: corner_down().wait_recv())
        pl.when(has_down)(lambda: row_up().wait_recv())
        pl.when(has_down)(lambda: corner_up().wait_recv())

    lifts = rows // 2 - 1
    span = crows // 2
    after = {}

    def book(at, call, rank=-1):
        after.setdefault(at, []).append((rank, call))

    for s in range(1, lifts):
        for g in range(1, groups):
            if (4 + 2 * (s - 1)) // per < g <= (4 + 2 * s) // per:
                book(s - 1, functools.partial(join_edges, g))
    book(lifts - 2, last_layers)
    for c in range(chunks):
        at = min((c + 1) * span - 1, lifts) if c < chunks - 1 else lifts
        due = lifts + c * span
        for call, later in zip((to_twin, to_peers, mix_chunk, forward), LATER[c]):
            place = min(at + later, due)
            rank = 2 * RANKS[call.__name__] + 6 * (call is to_peers and place == at)
            book(place, functools.partial(call, c), rank)

    def then(at):
        calls = after.get(at, [])
        if chunks > 1:
            calls = sorted(calls, key=lambda c: c[0])
        for _, call in calls:
            call()

    def lift_step(s, first, last):
        if not first:
            modes_two(2 * s + 1)
        lift_two(2 * s + 3)
        if last:
            modes_two(2 * s + 3)

    mix_weights()
    if chunks > 1:
        for s in range(lifts):
            lift_step(s, s % span == 0, s % span == span - 1)
            then(s)
        if lifts % span:
            modes_two(2 * lifts + 1)
    else:
        lift_step(0, True, False)
        then(0)

        @pl.loop(1, lifts)
        def _(s):
            lift_step(s, False, False)
            for at in range(1, lifts):
                if at in after:
                    pl.when(s == at)(lambda at=at: then(at))

        modes_two(2 * lifts + 1)
    lift_last()
    modes_of(rows - 1, rows - 2)
    modes_of(0, rows - 1)
    then(lifts)

    def arrive(c):
        fw_copy(c, 1 - core).wait_recv()

    arrive(0)
    blend(0, blend_a)
    widen(blend_a, gate_a)
    blend(1, blend_b)
    then(lifts + 1)

    @pl.loop(1, rows // 2)
    def _(s):
        if chunks > 1:
            pl.when(lax.rem(s, span) == 0)(lambda: arrive(s // span))
        t = 2 * s
        for p in range(pairs):
            widen(blend_b, gate_b, [p])
            narrow(t - 2, blend_a, gate_a, [p])
        blend(t, blend_a)
        for p in range(pairs):
            widen(blend_a, gate_a, [p])
            narrow(t - 1, blend_b, gate_b, [p])
        blend(t + 1, blend_b)
        for at in range(1, rows // 2):
            if lifts + 1 + at in after:
                pl.when(s == at)(lambda at=at: then(lifts + 1 + at))

    narrow(rows - 2, blend_a, gate_a)
    widen(blend_b, gate_b)
    narrow(rows - 1, blend_b, gate_b)

    pl.when(has_up)(lambda: row_up().wait_send())
    pl.when(has_down)(lambda: row_down().wait_send())
    pl.when(has_up)(lambda: corner_up().wait_send())
    pl.when(has_down)(lambda: corner_down().wait_send())
    for g in range(groups):
        pl.when(has_left)(lambda g=g: side_left(g).wait_send())
        pl.when(has_right)(lambda g=g: side_right(g).wait_send())
    for c in range(chunks):
        tw_copy(c).wait_send()
        fw_copy(c, core).wait_send()

        @pl.loop(1, chips)
        def _(o):
            rs_copy(c, o).wait_send()
            ag_copy(c, o).wait_send()


def per_device(n, m, field, conv_w, spec_re, spec_im, mlp_in, mlp_out):
    rows, depth, ch, width = field.shape
    modes = spec_re.shape[0]
    pairs = depth // 2
    total_groups = rows * pairs // PACK
    chunks = min(4, total_groups // n)
    share = total_groups // chunks // n
    groups = 2 * rows * depth // width
    dma = pltpu.SemaphoreType.DMA
    hbm = pl.BlockSpec(memory_space=pltpu.HBM)
    tile = (2 * ch, PACK * 2 * modes)
    result = pl.pallas_call(
        functools.partial(kernel, n, m, chunks),
        out_shape=pltpu.VMEM((rows, pairs, 2 * ch, width), BF16),
        in_specs=[hbm] * 6,
        out_specs=pl.BlockSpec(memory_space=pltpu.VMEM),
        scratch_shapes=[
            pltpu.VMEM((rows + 2, depth + 2, ch, width), BF16),
            pltpu.VMEM((2, depth + 2, ch, width), BF16),
            pltpu.VMEM((2, depth + 2, ch, width), BF16),
            pltpu.VMEM((depth // 4, 2 * ch, 2 * width), F32),
            pltpu.VMEM((depth // 4, 2 * ch, 2 * width), F32),
            pltpu.VMEM((depth // 4, 2 * ch, 2 * width), F32),
            pltpu.VMEM((rows, pairs, 2 * ch, width), BF16),
            pltpu.VMEM((groups, ch, width), BF16),
            pltpu.VMEM((2, groups, ch, width), BF16),
            pltpu.VMEM((groups + 2, ch, width), BF16),
            pltpu.VMEM((mlp_in.shape[0], ch), BF16),
            pltpu.VMEM(mlp_out.shape, BF16),
            pltpu.VMEM((6 * ch, 12 * ch), BF16),
            pltpu.VMEM((modes, 2 * ch, 2 * ch), BF16),
            pltpu.VMEM((PACK * width, PACK * 2 * modes), BF16),
            pltpu.VMEM((2 * PACK * 2 * modes, PACK * width), BF16),
            pltpu.VMEM((total_groups,) + tile, BF16),
            pltpu.VMEM((chunks, total_groups // chunks // 2) + tile, BF16),
            pltpu.VMEM((chunks, total_groups // chunks // 2) + tile, BF16),
            pltpu.VMEM((chunks, n // 2, share) + tile, BF16),
            pltpu.VMEM((share,) + tile, F32),
            pltpu.VMEM((PACK * 2 * modes, 2 * ch), F32),
            pltpu.VMEM((total_groups,) + tile, BF16),
            pltpu.VMEM((pairs, 2 * ch, width), BF16),
            pltpu.VMEM((pairs, 2 * ch, width), BF16),
            pltpu.VMEM((pairs, mlp_in.shape[0], 2 * width), BF16),
            pltpu.VMEM((pairs, mlp_in.shape[0], 2 * width), BF16),
            pltpu.VMEM(conv_w.shape, BF16),
            pltpu.VMEM(spec_re.shape, F32),
            pltpu.VMEM(spec_im.shape, F32),
            pltpu.VMEM(mlp_in.shape[::-1], BF16),
            pltpu.VMEM(mlp_out.shape, BF16),
            dma((rows,)), dma((5,)),
            dma((2,)), dma((2,)),
            dma((2, groups)), dma((2, groups)),
            dma((2,)), dma((2,)),
            dma((chunks,)), dma((chunks,)),
            dma((chunks, n // 2)), dma((chunks, n // 2)),
            dma((chunks, n // 2)), dma((chunks, n // 2)),
            dma((chunks,)), dma((chunks,)),
        ],
        compiler_params=pltpu.CompilerParams(
            collective_id=0, has_side_effects=True, vmem_limit_bytes=59 << 20
        ),
    )(field, conv_w, spec_re, spec_im, mlp_in.T, mlp_out)
    return result.reshape(rows, depth, ch, width)


def solution(mesh):
    in_specs = (P("gy", None, None, "gx"), P(), P(), P(), P(), P())
    out_specs = P("gy", None, None, "gx")
    return jax.shard_map(
        functools.partial(per_device, mesh.shape["gx"], mesh.shape["gy"]),
        mesh=mesh, in_specs=in_specs, out_specs=out_specs, check_vma=False,
    )
```
